128 devices in a mesh: dp: 4 (over z), context: 4 (over y), tensor: 8 (over x, core).
Axes of the slice: x: 4, y: 4, z: 4, core: 2. Of those that a mesh axis runs over, the one named last changes fastest.
Arguments:
- inputs: bfloat16 [8192, 5376], P(('dp', 'context')), may hold values from -8 to 8
- queries: bfloat16 [8192, 2048], P(('dp', 'context'), 'tensor'), may hold values from -8 to 8
- key_states: bfloat16 [8192, 1024], P(('dp', 'context'), 'tensor'), may hold values from -8 to 8
- value_states: bfloat16 [8192, 1024], P(('dp', 'context'), 'tensor'), may hold values from -6 to 6
- out_grad: bfloat16 [8192, 5376], P(('dp', 'context')), may hold values from -8 to 8
- positions: int32 [8192], P(('dp', 'context')), may hold values from 0 to 10239, as said below
- w_query: bfloat16 [5376, 2048], P(None, 'tensor'), may hold values from -0.078125 to 0.078125
- w_key: bfloat16 [5376, 1024], P(None, 'tensor'), may hold values from -0.078125 to 0.078125
- w_value: bfloat16 [5376, 1024], P(None, 'tensor'), may hold values from -0.078125 to 0.078125
- w_output: bfloat16 [5376, 2048], P(None, 'tensor'), may hold values from -0.125 to 0.125
Outputs:
- input_grad: bfloat16 [8192, 5376], P(('dp', 'context', 'tensor'))
- grad_query: float32 [5376, 2048], P(('dp', 'context'), 'tensor')
- grad_key: float32 [5376, 1024], P(('dp', 'context'), 'tensor')
- grad_value: float32 [5376, 1024], P(('dp', 'context'), 'tensor')
- grad_output: float32 [5376, 2048], P(('dp', 'context'), 'tensor')
The draws below stay inside these ranges and needn't reach their ends.
Inputs may be any that keep to these rules, and one draw needn't show every extreme that they name: Within a document positions rise by one from token to token; a position of 0 starts a new document; the first document of each replica's 2048 tokens may have begun before them.
All inputs are finite; a program needn't handle non-finite values.
Results may differ from the reference program's by a relative error of at most 0.02.
Values may be sent and summed in bfloat16 or wider, within the bound.
A program may use at most 128 MiB of HBM per device.

```python
import jax
import jax.numpy as jnp
from jax import lax

D = 5376
H = 16
KVH = 8
HD = 128
W = 1024
QSCALAR = 168
SEG = 2048
TOKENS = 8192


def build_positions(key):
    base = jax.random.fold_in(key, 7)
    replicas = TOKENS // SEG
    replica_index = jnp.arange(replicas, dtype=jnp.int32)[:, None]
    index = jnp.broadcast_to(jnp.arange(SEG, dtype=jnp.int32)[None, :], (replicas, SEG))
    breaks = jax.random.randint(jax.random.fold_in(base, 1), (replicas, SEG), 0, W) == 0
    breaks = breaks & (replica_index >= 1)
    forced = (replica_index == replicas - 1) & (index == SEG // 2)
    breaks = breaks | forced
    offsets = jax.random.randint(jax.random.fold_in(base, 2), (replicas,), 0, 8 * W)
    offsets = offsets.at[0].set(8 * W)
    marker = jnp.where(breaks, index, -16 * W)
    opening = jnp.where(breaks[:, 0], 0, -offsets).astype(jnp.int32)
    marker = marker.at[:, 0].set(opening)
    latest = lax.cummax(marker, axis=1)
    return (index - latest).reshape(TOKENS).astype(jnp.int32)


def draw_positions(key, part):
    return build_positions(key)


def draw_key_states(key, part):
    base = jax.random.normal(jax.random.fold_in(key, 21), (TOKENS, KVH * HD), jnp.float32)
    return jnp.clip(base, -6.0, 6.0).astype(jnp.bfloat16)


def draw_queries(key, part):
    base = jax.random.normal(jax.random.fold_in(key, 31), (TOKENS, H * HD), jnp.float32)
    return jnp.clip(base, -6.0, 6.0).astype(jnp.bfloat16)


def spiked(values, key, source, target, blocks, factor):
    def block_of(axis_at):
        return (jnp.arange(values.shape[axis_at]) // (values.shape[axis_at] // blocks)).reshape((-1,) + (1,) * (values.ndim - 1 - axis_at))

    first = jax.random.permutation(key, blocks)[block_of(target)]
    far = (block_of(target) + blocks // 2) % blocks
    return jnp.where((block_of(source) == first) | (block_of(source) == far), factor * values, values)


def block_scale(stream_key, extent, cuts, low, high):
    factor_of = 1.0
    for dim, blocks in cuts:
        draws = jax.random.uniform(jax.random.fold_in(jax.random.fold_in(stream_key, 6), dim), (blocks,), jnp.float32, low / len(cuts), high / len(cuts))
        factor_of = factor_of * jnp.repeat(jnp.exp(draws), extent[dim] // blocks).reshape((-1,) + (1,) * (len(extent) - 1 - dim))
    return factor_of


def normal_values(key, dims, scale, reach, cuts=(), kind=jnp.bfloat16):
    result = jax.random.normal(key, dims, jnp.float32) * scale
    if len(cuts) > 0:
        result = block_scale(key, dims, cuts, -0.22, 0.18) * result
    return jnp.clip(result, min=-reach, max=reach).astype(kind)


def bell_draw_with(own_key, shape, scale, reach, shards, heavy, kind=jnp.bfloat16):
    values = scale * jax.random.normal(own_key, shape, jnp.float32)
    if shards:
        values = values * block_scale(own_key, shape, shards, -0.22, 0.18)
    return jnp.clip(spiked(values, jax.random.fold_in(own_key, 3), *heavy), -reach, reach).astype(kind)


def setup_inputs(seed: int = 0) -> dict:
    arg_keys = jax.random.split(jax.random.key(seed), 11)
    inputs = bell_draw_with(arg_keys[0], (TOKENS, D), 1.0, 8.0, ((0, 16),), (0, 1, 16, 2.0))
    queries = draw_queries(jax.random.fold_in(arg_keys[10], 71), 0)
    key_states = draw_key_states(jax.random.fold_in(arg_keys[10], 71), 0)
    value_states = normal_values(arg_keys[3], (TOKENS, KVH * HD), 1.0, 6.0, ((0, 16), (1, 8)))
    out_grad = bell_draw_with(arg_keys[4], (TOKENS, D), 1.0, 8.0, ((0, 16),), (0, 1, 16, 2.0))
    positions = draw_positions(jax.random.fold_in(arg_keys[10], 71), 0)
    w_query = normal_values(arg_keys[6], (D, H * HD), D ** -0.5, 0.078125, ((1, 8),))
    w_key = normal_values(arg_keys[7], (D, KVH * HD), D ** -0.5, 0.078125, ((1, 8),))
    w_value = normal_values(arg_keys[8], (D, KVH * HD), D ** -0.5, 0.078125, ((1, 8),))
    w_output = normal_values(arg_keys[9], (D, H * HD), (H * HD) ** -0.5, 0.125, ((1, 8),))
    return dict(inputs=inputs, queries=queries, key_states=key_states, value_states=value_states, out_grad=out_grad, positions=positions, w_query=w_query, w_key=w_key, w_value=w_value, w_output=w_output)


def rotate_back(grads, places):
    count = grads.shape[0]
    half = HD // 2
    index = jnp.arange(half, dtype=jnp.float32)
    freq = jnp.power(jnp.float32(10000.0), index * (-2.0 / HD))
    angle = places.astype(jnp.float32)[:, None] * freq[None, :]
    cosine = jnp.cos(angle)[:, None, :]
    sine = jnp.sin(angle)[:, None, :]
    split = grads.reshape(count, -1, 2, half)
    first = split[:, :, 0, :]
    second = split[:, :, 1, :]
    upper = first * cosine + second * sine
    lower = second * cosine - first * sine
    return jnp.stack([upper, lower], axis=2).reshape(count, -1)


def group_backward(query_group, key_group, value_group, dattn_group, allowed):
    scale = QSCALAR ** -0.5
    query_wide = query_group.astype(jnp.float32)
    key_wide = key_group.astype(jnp.float32)
    value_wide = value_group.astype(jnp.float32)
    dattn_wide = dattn_group.astype(jnp.float32)
    scores = jnp.einsum("gqd,kd->gqk", query_wide, key_wide) * scale
    scores = jnp.where(allowed[None], scores, -1e30)
    top = jnp.max(scores, axis=-1, keepdims=True)
    weights = jnp.exp(scores - top)
    probs = weights / jnp.sum(weights, axis=-1, keepdims=True)
    probs_half = probs.astype(jnp.bfloat16)
    attn = jnp.einsum("gqk,kd->gqd", probs_half.astype(jnp.float32), value_wide).astype(jnp.bfloat16)
    dprobs = jnp.einsum("gqd,kd->gqk", dattn_wide, value_wide)
    delta = jnp.sum(dattn_wide * attn.astype(jnp.float32), axis=-1, keepdims=True)
    dscores = (probs * (dprobs - delta) * scale).astype(jnp.bfloat16)
    dscores_wide = dscores.astype(jnp.float32)
    query_grad = jnp.einsum("gqk,kd->gqd", dscores_wide, key_wide)
    key_grad = jnp.einsum("gqk,gqd->kd", dscores_wide, query_wide)
    value_grad = jnp.einsum("gqk,gqd->kd", probs_half.astype(jnp.float32), dattn_wide)
    return attn, query_grad, key_grad, value_grad


def reference(inputs, queries, key_states, value_states, out_grad, positions, w_query, w_key, w_value, w_output):
    group = H // KVH
    index = jnp.arange(SEG, dtype=jnp.int32)
    input_parts = []
    grad_sums = None
    for replica in range(TOKENS // SEG):
        first_row = replica * SEG
        input_rows = inputs[first_row:first_row + SEG]
        query_rows = queries[first_row:first_row + SEG]
        key_rows = key_states[first_row:first_row + SEG]
        value_rows = value_states[first_row:first_row + SEG]
        grad_rows = out_grad[first_row:first_row + SEG]
        places = positions[first_row:first_row + SEG]
        starts = index - places
        allowed = (index[None, :] <= index[:, None]) & (index[:, None] - index[None, :] < W) & (index[None, :] >= starts[:, None])
        dattn = jnp.dot(grad_rows, w_output, preferred_element_type=jnp.float32).astype(jnp.bfloat16)
        query_heads = query_rows.reshape(SEG, KVH, group, HD).transpose(1, 2, 0, 3)
        dattn_heads = dattn.reshape(SEG, KVH, group, HD).transpose(1, 2, 0, 3)
        key_heads = key_rows.reshape(SEG, KVH, HD).transpose(1, 0, 2)
        value_heads = value_rows.reshape(SEG, KVH, HD).transpose(1, 0, 2)

        def one_group(parts):
            return group_backward(parts[0], parts[1], parts[2], parts[3], allowed)

        attn, query_grad, key_grad, value_grad = lax.map(one_group, (query_heads, key_heads, value_heads, dattn_heads))
        attn_flat = attn.transpose(2, 0, 1, 3).reshape(SEG, H * HD)
        query_flat = query_grad.transpose(2, 0, 1, 3).reshape(SEG, H * HD)
        key_flat = key_grad.transpose(1, 0, 2).reshape(SEG, KVH * HD)
        value_flat = value_grad.transpose(1, 0, 2).reshape(SEG, KVH * HD)
        query_lin = rotate_back(query_flat, places).astype(jnp.bfloat16)
        key_lin = rotate_back(key_flat, places).astype(jnp.bfloat16)
        value_half = value_flat.astype(jnp.bfloat16)
        input_grad = jnp.dot(query_lin, w_query.T, preferred_element_type=jnp.float32)
        input_grad = input_grad + jnp.dot(key_lin, w_key.T, preferred_element_type=jnp.float32)
        input_grad = input_grad + jnp.dot(value_half, w_value.T, preferred_element_type=jnp.float32)
        input_parts.append(input_grad.astype(jnp.bfloat16))
        terms = (jnp.dot(input_rows.T, query_lin, preferred_element_type=jnp.float32),
                 jnp.dot(input_rows.T, key_lin, preferred_element_type=jnp.float32),
                 jnp.dot(input_rows.T, value_half, preferred_element_type=jnp.float32),
                 jnp.dot(grad_rows.T, attn_flat, preferred_element_type=jnp.float32))
        if grad_sums is None:
            grad_sums = terms
        else:
            grad_sums = tuple(old + new for old, new in zip(grad_sums, terms))
    return (jnp.concatenate(input_parts, axis=0), grad_sums[0], grad_sums[1], grad_sums[2], grad_sums[3])
```

```python
import functools

import jax
import jax.numpy as jnp
from jax import lax
from jax.experimental import pallas as pl
from jax.experimental.pallas import tpu as pltpu
from jax.sharding import PartitionSpec as P

HD = 128
W = 1024
QSCALAR = 168
D = 5376
ROWS = 512
TILE = 128
WINDOW = W + TILE
BAND = 3 * ROWS
OWN = D // 16
HALF = D // 2
TOP = 176
CHUNK = 384
F32 = jnp.float32
BF16 = jnp.bfloat16
MESH = pl.DeviceIdType.MESH


def nt(left, right):
    return lax.dot_general(left, right, (((1,), (1,)), ((), ())), preferred_element_type=F32)


def nn(left, right):
    return jnp.dot(left, right, preferred_element_type=F32)


def rotate(grad, cosine, sine):
    return grad * cosine + pltpu.roll(grad, HD // 2, 1) * sine


def attention_kernel(
    q_ref, k_ref, v_ref, dattn_ref, lo_ref, cos_ref, sin_ref,
    attn_ref, qlin_ref, own_ref, away_ref, dkt, dvt,
):
    scale = QSCALAR ** (-0.5)
    dkt[...] = jnp.zeros_like(dkt)
    dvt[...] = jnp.zeros_like(dvt)

    def tile(t, carry):
        base = pl.multiple_of(t * TILE, TILE)
        rows = pl.ds(base, TILE)
        wide = pl.ds(base, WINDOW)
        query = jnp.concatenate([q_ref[rows, :HD], q_ref[rows, HD:]], axis=0)
        dattn = jnp.concatenate([dattn_ref[rows, :HD], dattn_ref[rows, HD:]], axis=0)
        keys = k_ref[wide, :]
        values = v_ref[wide, :]
        low = lo_ref[rows, :] - base
        low = jnp.concatenate([low, low], axis=0)
        row = lax.broadcasted_iota(jnp.int32, (2 * TILE, 1), 0) % TILE
        col = lax.broadcasted_iota(jnp.int32, (2 * TILE, WINDOW), 1)
        allowed = (col >= low) & (col <= row + W)
        scores = jnp.where(allowed, nt(query, keys) * scale, -1e30)
        top = jnp.max(scores, axis=-1, keepdims=True)
        weights = jnp.exp(scores - top)
        probs = weights / jnp.sum(weights, axis=-1, keepdims=True)
        half = probs.astype(BF16)
        attn = nn(half, values).astype(BF16)
        attn_ref[rows, :HD] = attn[:TILE]
        attn_ref[rows, HD:] = attn[TILE:]
        dprobs = nt(dattn, values)
        delta = jnp.sum(dattn.astype(F32) * attn.astype(F32), axis=-1, keepdims=True)
        dscores = (probs * (dprobs - delta) * scale).astype(BF16)
        dq = nn(dscores, keys)
        qlin_ref[rows, :HD] = rotate(dq[:TILE], cos_ref[rows, :], sin_ref[rows, :]).astype(BF16)
        qlin_ref[rows, HD:] = rotate(dq[TILE:], cos_ref[rows, :], sin_ref[rows, :]).astype(BF16)
        dkt[:, wide] += nn(query.T, dscores)
        dvt[:, wide] += nn(dattn.T, half)
        return carry

    lax.fori_loop(0, ROWS // TILE, tile, 0)
    for kind, total in enumerate((dkt, dvt)):
        own_ref[kind] = total[:, 2 * ROWS :].T
        away_ref[0, kind] = total[:, ROWS : 2 * ROWS].T.astype(BF16)
        away_ref[1, kind] = total[:, :ROWS].T.astype(BF16)


def attention(q, k, v, dattn, low, cosine, sine):
    vmem = pl.BlockSpec(memory_space=pltpu.VMEM)
    return pl.pallas_call(
        attention_kernel,
        out_shape=(
            jax.ShapeDtypeStruct((ROWS, 2 * HD), BF16),
            jax.ShapeDtypeStruct((ROWS, 2 * HD), BF16),
            jax.ShapeDtypeStruct((2, ROWS, HD), F32),
            jax.ShapeDtypeStruct((2, 2, ROWS, HD), BF16),
        ),
        in_specs=[vmem] * 7,
        out_specs=(vmem,) * 4,
        scratch_shapes=[pltpu.VMEM((HD, BAND), F32), pltpu.VMEM((HD, BAND), F32)],
        compiler_params=pltpu.CompilerParams(vmem_limit_bytes=40 << 20),
        name="attention",
    )(q, k, v, dattn, low, cosine, sine)


def step(axis, index, delta):
    size = 4
    return {axis: lax.rem(index + delta + size, size)}


def reduce_kernel(
    x_hbm, og_hbm, wq_hbm, wk_hbm, wv_hbm, attn_ref, qlin_ref, kv_ref,
    ig_out, gq_out, gk_out, gv_out, go_out,
    x_buf, og_buf, xt, wq, wk, wv, parts, mids, near, far, ig, pair, xring, load_sem,
    c_send, c_recv, e_send, e_recv, f_send, f_recv, g_send, g_recv,
):
    z = lax.axis_index("dp")
    y = lax.axis_index("context")
    t = lax.axis_index("tensor")
    core = lax.rem(t, 2)
    chip = t // 2
    partner = {"tensor": t + 1 - 2 * core}
    xplus = {"tensor": lax.rem(t + 2, 8)}
    xminus = {"tensor": lax.rem(t + 6, 8)}
    loads = [
        pltpu.make_async_copy(src, dst, load_sem.at[i])
        for i, (src, dst) in enumerate(
            ((og_hbm, og_buf), (x_hbm, x_buf), (wq_hbm, wq), (wk_hbm, wk), (wv_hbm, wv))
        )
    ]
    for load in loads:
        load.start()
    barrier = pltpu.get_barrier_semaphore()
    ids = [step("dp", z, 1), step("dp", z, -1), step("context", y, 1), step("context", y, -1)]
    for device in ids + [xplus, xminus, partner]:
        pl.semaphore_signal(barrier, inc=1, device_id=device, device_id_type=MESH)
    pl.semaphore_wait(barrier, 7)

    lines = (("dp", z, "context", y), ("context", y, "dp", z))

    def remote(src, dst, send, recv, device):
        return pltpu.make_async_remote_copy(
            src_ref=src, dst_ref=dst, send_sem=send, recv_sem=recv,
            device_id=device, device_id_type=MESH,
        )

    @functools.cache
    def outer(r, kind):
        axis, me, _, _ = lines[kind]
        there = 4 * lax.rem(me + 2, 4)
        after = 4 * lax.rem(me + 1, 4)
        before = 4 * lax.rem(me + 3, 4)
        up, down = step(axis, me, 1), step(axis, me, -1)
        part = parts.at[r, kind]
        plan = (
            (there, up), (there + 2, down), (after + 2, up), (before, down),
            (after, up), (before + 2, down),
        )
        return [
            remote(
                part.at[pl.ds(start, 2)], near.at[r, kind, n],
                c_send.at[r, kind, n], c_recv.at[r, kind, n], device,
            )
            for n, (start, device) in enumerate(plan)
        ]

    @functools.cache
    def inner(r, kind):
        _, _, axis, me = lines[kind]
        there = lax.rem(me + 2, 4)
        after = lax.rem(me + 1, 4)
        before = lax.rem(me + 3, 4)
        up, down = step(axis, me, 1), step(axis, me, -1)
        upper, lower = pl.ds(0, TOP), pl.ds(TOP, OWN - TOP)
        mid = mids.at[r, kind]
        plan = (
            (there, upper, up), (there, lower, down), (after, lower, up), (before, upper, down),
            (after, upper, up), (before, lower, down),
        )
        return [
            remote(
                mid.at[block, rows], far.at[r, kind, n, pl.ds(0, rows.size)],
                e_send.at[r, kind, n], e_recv.at[r, kind, n], device,
            )
            for n, (block, rows, device) in enumerate(plan)
        ]

    def transpose(src):
        def body(i, carry):
            lanes = pl.ds(pl.multiple_of(i * 128, 128), 128)
            xt[lanes, :] = src[:, lanes].T
            return carry

        lax.fori_loop(0, D // 128, body, 0)

    def multiply(r, right_ref):
        right = right_ref[...]

        def body(o, carry):
            rows = pl.ds(pl.multiple_of(o * OWN, 16), OWN)
            product = nn(xt[rows, :], right).astype(BF16)
            parts[r, 0, o] = product[:, :HD]
            parts[r, 1, lax.rem(o, 4) * 4 + o // 4] = product[:, HD:]
            return carry

        lax.fori_loop(0, 16, body, 0)

    def outer_first(r):
        copies = [outer(r, kind) for kind in range(2)]
        for n in range(4):
            for kind in range(2):
                copies[kind][n].start()

    def outer_second(r):
        for kind in range(2):
            me = lines[kind][1]
            after = 4 * lax.rem(me + 1, 4)
            before = 4 * lax.rem(me + 3, 4)
            copies = outer(r, kind)
            for n, start in ((0, after), (1, before + 2)):
                copies[n].wait_recv()
                where = pl.ds(start, 2)
                parts[r, kind, where] = (
                    parts[r, kind, where].astype(F32) + near[r, kind, n].astype(F32)
                ).astype(BF16)
                copies[4 + n].start()

    outs = ((go_out, go_out), (gq_out, gq_out), (gk_out, gv_out))

    def target(r, kind):
        out = outs[r][kind]
        lanes = pl.ds(HD * kind, HD) if r < 2 else pl.ds(0, HD)
        return out, lanes

    def outer_sum(r, kind, block):
        me = lines[kind][1]
        own = parts[r, kind, 4 * me + block].astype(F32)
        first, second = (4, 3) if block < 2 else (2, 5)
        within = block % 2
        return (
            own + near[r, kind, first, within].astype(F32)
            + near[r, kind, second, within].astype(F32)
        )

    def inner_first(r):
        for kind in range(2):
            copies = outer(r, kind)
            for n in (2, 3, 4, 5):
                copies[n].wait_recv()
            for block in range(4):
                mids[r, kind, block] = outer_sum(r, kind, block)[...].astype(BF16)
            sends = inner(r, kind)
            for n in range(4):
                sends[n].start()

    def inner_second(r):
        for kind in range(2):
            me = lines[kind][3]
            after = lax.rem(me + 1, 4)
            before = lax.rem(me + 3, 4)
            copies = inner(r, kind)
            for n, block, rows in (
                (0, after, pl.ds(0, TOP)), (1, before, pl.ds(TOP, OWN - TOP)),
            ):
                copies[n].wait_recv()
                mids[r, kind, block, rows] = (
                    mids[r, kind, block, rows].astype(F32)
                    + far[r, kind, n, pl.ds(0, rows.size)].astype(F32)
                ).astype(BF16)
                copies[4 + n].start()

    def inner_last(r):
        for kind in range(2):
            me = lines[kind][3]
            copies = inner(r, kind)
            for n in (2, 3, 4, 5):
                copies[n].wait_recv()
            out, lanes = target(r, kind)
            for rows, first, second in (
                (pl.ds(0, TOP), 4, 3), (pl.ds(TOP, OWN - TOP), 2, 5),
            ):
                size = pl.ds(0, rows.size)
                out[rows, lanes] = (
                    mids[r, kind, me, rows].astype(F32)
                    + far[r, kind, first, size].astype(F32)
                    + far[r, kind, second, size].astype(F32)
                )

    there, after, before = lax.rem(chip + 2, 4), lax.rem(chip + 1, 4), lax.rem(chip + 3, 4)

    @functools.cache
    def pair_copies():
        return [
            remote(
                ig.at[1 - core, block], pair.at[block], f_send.at[n], f_recv.at[n], partner
            )
            for n, block in enumerate((there, after, before, chip))
        ]

    @functools.cache
    def ring_copies():
        mine = ig.at[core]
        plan = (
            (there, 0, xplus), (there, 1, xminus), (after, 1, xplus), (before, 0, xminus),
            (after, 0, xplus), (before, 1, xminus),
        )
        return [
            remote(mine.at[block, h], xring.at[n], g_send.at[n], g_recv.at[n], device)
            for n, (block, h, device) in enumerate(plan)
        ]

    def input_multiply():
        query, key, value = qlin_ref[...], kv_ref[:, :HD], kv_ref[:, HD:]
        for h in range(2):
            def body(i, carry, h=h):
                rows = pl.ds(pl.multiple_of(h * HALF + i * CHUNK, 128), CHUNK)
                lanes = pl.ds(pl.multiple_of(i * CHUNK, 128), CHUNK)
                total = nt(query, wq[rows, :]) + nt(key, wk[rows, :]) + nt(value, wv[rows, :])
                total = total.astype(BF16)
                for o in range(8):
                    ig[o % 2, o // 2, h, :, lanes] = total[64 * o : 64 * o + 64]
                return carry

            lax.fori_loop(0, HALF // CHUNK, body, 0)

    def pair_add():
        copies = pair_copies()
        sends = ring_copies()
        for n, block in enumerate((there, after, before, chip)):
            copies[n].wait_recv()
            for h in range(2):
                ig[core, block, h] = (
                    ig[core, block, h].astype(F32) + pair[block, h].astype(F32)
                ).astype(BF16)
            for m in ((0, 1), (2,), (3,), ())[n]:
                sends[m].start()

    def ring_second():
        copies = ring_copies()
        for n, block in ((0, after), (1, before)):
            copies[n].wait_recv()
            ig[core, block, n] = (
                ig[core, block, n].astype(F32) + xring[n].astype(F32)
            ).astype(BF16)
            copies[4 + n].start()

    def ring_last():
        copies = ring_copies()
        for n in (2, 3, 4, 5):
            copies[n].wait_recv()
        for h, first, second in ((0, 4, 3), (1, 2, 5)):
            ig_out[:, pl.ds(h * HALF, HALF)] = (
                ig[core, chip, h].astype(F32) + xring[first].astype(F32)
                + xring[second].astype(F32)
            ).astype(BF16)

    loads[0].wait()
    transpose(og_buf)
    multiply(0, attn_ref)
    outer_first(0)
    loads[1].wait()
    transpose(x_buf)
    multiply(1, qlin_ref)
    outer_first(1)
    multiply(2, kv_ref)
    outer_first(2)
    for load in loads[2:]:
        load.wait()
    input_multiply()
    for copy in pair_copies():
        copy.start()
    outer_second(0)
    pair_add()
    outer_second(1)
    inner_first(0)
    outer_second(2)
    ring_second()
    inner_second(0)
    inner_first(1)
    inner_second(1)
    inner_last(0)
    inner_first(2)
    inner_second(2)
    ring_last()
    inner_last(1)
    inner_last(2)
    for r in range(3):
        for kind in range(2):
            for copy in outer(r, kind) + inner(r, kind):
                copy.wait_send()
    for copy in pair_copies() + ring_copies():
        copy.wait_send()


def reduce_all(x, og, wq, wk, wv, attn, qlin, kv):
    vmem = pl.BlockSpec(memory_space=pltpu.VMEM)
    anywhere = pl.BlockSpec(memory_space=pl.ANY)
    dma = pltpu.SemaphoreType.DMA
    return pl.pallas_call(
        reduce_kernel,
        out_shape=(
            jax.ShapeDtypeStruct((64, D), BF16),
            jax.ShapeDtypeStruct((OWN, 2 * HD), F32),
            jax.ShapeDtypeStruct((OWN, HD), F32),
            jax.ShapeDtypeStruct((OWN, HD), F32),
            jax.ShapeDtypeStruct((OWN, 2 * HD), F32),
        ),
        in_specs=[anywhere] * 5 + [vmem] * 3,
        out_specs=(vmem,) * 5,
        scratch_shapes=[
            pltpu.VMEM((ROWS, D), BF16),
            pltpu.VMEM((ROWS, D), BF16),
            pltpu.VMEM((D, ROWS), BF16),
            pltpu.VMEM((D, 2 * HD), BF16),
            pltpu.VMEM((D, HD), BF16),
            pltpu.VMEM((D, HD), BF16),
            pltpu.VMEM((3, 2, 16, OWN, HD), BF16),
            pltpu.VMEM((3, 2, 4, OWN, HD), BF16),
            pltpu.VMEM((3, 2, 6, 2, OWN, HD), BF16),
            pltpu.VMEM((3, 2, 6, TOP, HD), BF16),
            pltpu.VMEM((2, 4, 2, 64, HALF), BF16),
            pltpu.VMEM((4, 2, 64, HALF), BF16),
            pltpu.VMEM((6, 64, HALF), BF16),
            dma((5,)),
            dma((3, 2, 6)), dma((3, 2, 6)), dma((3, 2, 6)), dma((3, 2, 6)),
            dma((4,)), dma((4,)), dma((6,)), dma((6,)),
        ],
        compiler_params=pltpu.CompilerParams(
            collective_id=0, has_side_effects=True, vmem_limit_bytes=60 << 20
        ),
        name="reduce_all",
    )(x, og, wq, wk, wv, attn, qlin, kv)


def on_device(
    inputs, queries, key_states, value_states, out_grad, positions,
    w_query, w_key, w_value, w_output,
):
    block = lax.axis_index("context")
    kv = jnp.concatenate([key_states, value_states], axis=1)
    ahead = [[(i, i + n) for i in range(4 - n)] for n in (1, 2)]
    back = [[(i + n, i) for i in range(4 - n)] for n in (1, 2)]
    middle = lax.ppermute(kv, "context", ahead[0])
    oldest = lax.ppermute(kv, "context", ahead[1])
    dattn = jnp.dot(out_grad, w_output, preferred_element_type=F32).astype(BF16)
    band = jnp.concatenate([oldest, middle, kv], axis=0)

    row = jnp.arange(ROWS, dtype=jnp.int32)
    index = block * ROWS + row
    low = jnp.maximum(jnp.maximum(index - (W - 1), index - positions), 0) - (block - 2) * ROWS
    order = jnp.arange(HD // 2, dtype=F32)
    freq = jnp.power(F32(10000.0), order * (-2.0 / HD))
    angle = positions.astype(F32)[:, None] * freq[None, :]
    cosine, sine = jnp.cos(angle), jnp.sin(angle)
    cosine = jnp.concatenate([cosine, cosine], axis=1)
    sine = jnp.concatenate([sine, -sine], axis=1)

    attn, qlin, own, away = attention(
        queries, band[:, :HD], band[:, HD:], dattn, low[:, None], cosine, sine
    )
    near = lax.ppermute(away[0], "context", back[0])
    far = lax.ppermute(away[1], "context", back[1])
    total = own + near.astype(F32) + far.astype(F32)
    key_grad = total[0]
    rolled = jnp.concatenate([key_grad[:, HD // 2 :], key_grad[:, : HD // 2]], axis=1)
    key_lin = (key_grad * cosine + rolled * sine).astype(BF16)
    kv_lin = jnp.concatenate([key_lin, total[1].astype(BF16)], axis=1)
    return reduce_all(inputs, out_grad, w_query, w_key, w_value, attn, qlin, kv_lin)


def solution(mesh):
    rows = ("dp", "context")
    return jax.shard_map(
        on_device,
        mesh=mesh,
        in_specs=(
            P(rows, None), P(rows, "tensor"), P(rows, "tensor"), P(rows, "tensor"),
            P(rows, None), P(rows), P(None, "tensor"), P(None, "tensor"),
            P(None, "tensor"), P(None, "tensor"),
        ),
        out_specs=(
            P(("dp", "context", "tensor"), None), P(rows, "tensor"), P(rows, "tensor"),
            P(rows, "tensor"), P(rows, "tensor"),
        ),
        check_vma=False,
    )
```

```python
import functools

import jax
import jax.numpy as jnp
from jax import lax
from jax.experimental import pallas as pl
from jax.experimental.pallas import tpu as pltpu
from jax.sharding import PartitionSpec as P

HD = 128
W = 1024
QSCALAR = 168
D = 5376
ROWS = 512
TILE = 128
WINDOW = W + TILE
BAND = 3 * ROWS
OWN = D // 16
HALF = D // 2
TOP = 176
F32 = jnp.float32
BF16 = jnp.bfloat16
MESH = pl.DeviceIdType.MESH


def nt(left, right):
    return lax.dot_general(left, right, (((1,), (1,)), ((), ())), preferred_element_type=F32)


def nn(left, right):
    return jnp.dot(left, right, preferred_element_type=F32)


def rotate(grad, cosine, sine):
    return grad * cosine + pltpu.roll(grad, HD // 2, 1) * sine


def step(axis, index, delta):
    size = 4
    return {axis: lax.rem(index + delta + size, size)}


def fused_kernel(
    q_ref, low_ref, cos_ref, sin_ref,
    k_hbm, v_hbm, x_hbm, og_hbm, wq_hbm, wk_hbm, wv_hbm, wo_hbm,
    ig_out, gq_out, gk_out, gv_out, go_out,
    keys, values, relay, act, weights, dattn, attn, lin, probs, dkt, dvt, gout, gin,
    parts, mids, near, far, ig, pair, xring, load_sem,
    a_send, a_recv, b_send, b_recv,
    c_send, c_recv, e_send, e_recv, f_send, f_recv, g_send, g_recv,
):
    scale = QSCALAR ** (-0.5)
    z = lax.axis_index("dp")
    y = lax.axis_index("context")
    t = lax.axis_index("tensor")
    core = lax.rem(t, 2)
    chip = t // 2
    partner = {"tensor": t + 1 - 2 * core}
    xplus = {"tensor": lax.rem(t + 2, 8)}
    xminus = {"tensor": lax.rem(t + 6, 8)}
    yplus, yminus = step("context", y, 1), step("context", y, -1)
    oldest, middle, latest = pl.ds(0, ROWS), pl.ds(ROWS, ROWS), pl.ds(2 * ROWS, ROWS)

    def load(n, src, dst):
        return pltpu.make_async_copy(src, dst, load_sem.at[n])

    load_og = load(0, og_hbm, act)
    load_wo = load(1, wo_hbm, weights.at[:, pl.ds(0, 2 * HD)])
    load_k = load(2, k_hbm, keys.at[latest])
    load_v = load(3, v_hbm, values.at[latest])
    load_x = load(4, x_hbm, act)
    load_w = [
        load(5 + n, src, weights.at[:, pl.ds(start, width)])
        for n, (src, start, width) in enumerate(
            ((wq_hbm, 0, 2 * HD), (wk_hbm, 2 * HD, HD), (wv_hbm, 3 * HD, HD))
        )
    ]
    for copy in (load_k, load_v, load_og, load_wo):
        copy.start()
    barrier = pltpu.get_barrier_semaphore()
    ids = [yplus, yminus, step("dp", z, 1), step("dp", z, -1), xplus, xminus, partner]
    for device in ids:
        pl.semaphore_signal(barrier, inc=1, device_id=device, device_id_type=MESH)
    pl.semaphore_wait(barrier, 7)

    lines = (("dp", z, "context", y), ("context", y, "dp", z))

    def remote(src, dst, send, recv, device):
        return pltpu.make_async_remote_copy(
            src_ref=src, dst_ref=dst, send_sem=send, recv_sem=recv,
            device_id=device, device_id_type=MESH,
        )

    @functools.cache
    def outer(r, kind):
        axis, me, _, _ = lines[kind]
        there = 4 * lax.rem(me + 2, 4)
        after = 4 * lax.rem(me + 1, 4)
        before = 4 * lax.rem(me + 3, 4)
        up, down = step(axis, me, 1), step(axis, me, -1)
        part = parts.at[r, kind]
        plan = (
            (there, up), (there + 2, down), (after + 2, up), (before, down),
            (after, up), (before + 2, down),
        )
        return [
            remote(
                part.at[pl.ds(start, 2)], near.at[r, kind, n],
                c_send.at[r, kind, n], c_recv.at[r, kind, n], device,
            )
            for n, (start, device) in enumerate(plan)
        ]

    @functools.cache
    def inner(r, kind):
        _, _, axis, me = lines[kind]
        there = lax.rem(me + 2, 4)
        after = lax.rem(me + 1, 4)
        before = lax.rem(me + 3, 4)
        up, down = step(axis, me, 1), step(axis, me, -1)
        upper, lower = pl.ds(0, TOP), pl.ds(TOP, OWN - TOP)
        mid = mids.at[r, kind]
        plan = (
            (there, upper, up), (there, lower, down), (after, lower, up), (before, upper, down),
            (after, upper, up), (before, lower, down),
        )
        return [
            remote(
                mid.at[block, rows], far.at[r, kind, n, pl.ds(0, rows.size)],
                e_send.at[r, kind, n], e_recv.at[r, kind, n], device,
            )
            for n, (block, rows, device) in enumerate(plan)
        ]

    def ring(n, src, dst, device):
        return remote(src, dst, a_send.at[n], a_recv.at[n], device)

    ring_kv = (
        ring(0, k_hbm, keys.at[middle], yplus),
        ring(1, v_hbm, relay, yminus),
        ring(2, v_hbm, values.at[middle], yplus),
        ring(3, keys.at[middle], keys.at[oldest], yplus),
        ring(4, relay, values.at[oldest], yminus),
    )

    def back(n, src, dst, device):
        return remote(gout.at[src] if src < 3 else gin.at[src - 3], gin.at[dst],
                      b_send.at[n], b_recv.at[n], device)

    ring_back = (
        back(0, 0, 0, yminus), back(1, 1, 1, yplus), back(2, 2, 2, yminus),
        back(3, 3, 3, yminus), back(4, 4, 4, yplus),
    )

    def stacked(ref, rows):
        return jnp.concatenate([ref[rows, :HD], ref[rows, HD:]], axis=0)

    def forward(i, carry):
        base = pl.multiple_of(i * TILE, TILE)
        rows = pl.ds(base, TILE)
        wide = pl.ds(base, WINDOW)
        low = low_ref[rows, :] - base
        low = jnp.concatenate([low, low], axis=0)
        row = lax.broadcasted_iota(jnp.int32, (2 * TILE, 1), 0) % TILE
        col = lax.broadcasted_iota(jnp.int32, (2 * TILE, WINDOW), 1)
        allowed = (col >= low) & (col <= row + W)
        scores = jnp.where(allowed, nt(stacked(q_ref, rows), keys[wide, :]) * scale, -1e30)
        top = jnp.max(scores, axis=-1, keepdims=True)
        raised = jnp.exp(scores - top)
        prob = raised / jnp.sum(raised, axis=-1, keepdims=True)
        probs[i] = prob
        result = nn(prob.astype(BF16), values[wide, :]).astype(BF16)
        attn[rows, :HD] = result[:TILE]
        attn[rows, HD:] = result[TILE:]
        return carry

    def backward(i, carry):
        base = pl.multiple_of(i * TILE, TILE)
        rows = pl.ds(base, TILE)
        wide = pl.ds(base, WINDOW)
        grad = stacked(dattn, rows)
        prob = probs[i]
        dprobs = nt(grad, values[wide, :])
        delta = jnp.sum(
            grad.astype(F32) * stacked(attn, rows).astype(F32), axis=-1, keepdims=True
        )
        dscores = (prob * (dprobs - delta) * scale).astype(BF16)
        dq = nn(dscores, keys[wide, :])
        lin[rows, :HD] = rotate(dq[:TILE], cos_ref[rows, :], sin_ref[rows, :]).astype(BF16)
        lin[rows, HD : 2 * HD] = rotate(
            dq[TILE:], cos_ref[rows, :], sin_ref[rows, :]
        ).astype(BF16)
        dkt[:, wide] += nn(stacked(q_ref, rows).T, dscores)
        dvt[:, wide] += nn(grad.T, prob.astype(BF16))
        return carry

    def multiply(r, right):
        def body(i, carry):
            lanes = pl.ds(pl.multiple_of(i * HALF, 128), HALF)
            product = lax.dot_general(
                act[:, lanes], right, (((0,), (0,)), ((), ())), preferred_element_type=F32
            ).astype(BF16)
            for j in range(8):
                rows = slice(OWN * j, OWN * j + OWN)
                parts[r, 0, 8 * i + j] = product[rows, :HD]
                parts[r, 1, 4 * (j % 4) + 2 * i + j // 4] = product[rows, HD:]
            return carry

        lax.fori_loop(0, 2, body, 0)

    def outer_first(r, kinds=(0, 1), order=(0, 1, 2, 3)):
        for n in order:
            for kind in kinds:
                outer(r, kind)[n].start()

    def outer_second(r, kinds=(0, 1)):
        for kind in kinds:
            me = lines[kind][1]
            after = 4 * lax.rem(me + 1, 4)
            before = 4 * lax.rem(me + 3, 4)
            copies = outer(r, kind)
            for n, start in ((0, after), (1, before + 2)):
                copies[n].wait_recv()
                where = pl.ds(start, 2)
                parts[r, kind, where] = (
                    parts[r, kind, where].astype(F32) + near[r, kind, n].astype(F32)
                ).astype(BF16)
                copies[4 + n].start()

    outs = ((go_out, go_out), (gq_out, gq_out), (gk_out, gv_out))

    def target(r, kind):
        out = outs[r][kind]
        lanes = pl.ds(HD * kind, HD) if r < 2 else pl.ds(0, HD)
        return out, lanes

    def outer_sum(r, kind, block):
        me = lines[kind][1]
        own = parts[r, kind, 4 * me + block].astype(F32)
        first, second = (4, 3) if block < 2 else (2, 5)
        within = block % 2
        return (
            own + near[r, kind, first, within].astype(F32)
            + near[r, kind, second, within].astype(F32)
        )

    def inner_first(r):
        for kind in range(2):
            copies = outer(r, kind)
            for n in (2, 3, 4, 5):
                copies[n].wait_recv()
            for block in range(4):
                mids[r, kind, block] = outer_sum(r, kind, block)[...].astype(BF16)
            sends = inner(r, kind)
            for n in range(4):
                sends[n].start()

    def inner_second(r):
        for kind in range(2):
            me = lines[kind][3]
            after = lax.rem(me + 1, 4)
            before = lax.rem(me + 3, 4)
            copies = inner(r, kind)
            for n, block, rows in (
                (0, after, pl.ds(0, TOP)), (1, before, pl.ds(TOP, OWN - TOP)),
            ):
                copies[n].wait_recv()
                mids[r, kind, block, rows] = (
                    mids[r, kind, block, rows].astype(F32)
                    + far[r, kind, n, pl.ds(0, rows.size)].astype(F32)
                ).astype(BF16)
                copies[4 + n].start()

    def inner_last(r):
        for kind in range(2):
            me = lines[kind][3]
            copies = inner(r, kind)
            for n in (2, 3, 4, 5):
                copies[n].wait_recv()
            out, lanes = target(r, kind)
            for rows, first, second in (
                (pl.ds(0, TOP), 4, 3), (pl.ds(TOP, OWN - TOP), 2, 5),
            ):
                size = pl.ds(0, rows.size)
                out[rows, lanes] = (
                    mids[r, kind, me, rows].astype(F32)
                    + far[r, kind, first, size].astype(F32)
                    + far[r, kind, second, size].astype(F32)
                )

    there, after, before = lax.rem(chip + 2, 4), lax.rem(chip + 1, 4), lax.rem(chip + 3, 4)

    @functools.cache
    def pair_copies():
        return [
            remote(
                ig.at[1 - core, block], pair.at[block], f_send.at[n], f_recv.at[n], partner
            )
            for n, block in enumerate((there, after, before, chip))
        ]

    @functools.cache
    def ring_copies():
        mine = ig.at[core]
        plan = (
            (there, 0, xplus), (there, 1, xminus), (after, 1, xplus), (before, 0, xminus),
            (after, 0, xplus), (before, 1, xminus),
        )
        return [
            remote(mine.at[block, h], xring.at[n], g_send.at[n], g_recv.at[n], device)
            for n, (block, h, device) in enumerate(plan)
        ]

    def input_multiply():
        for h in range(2):
            total = nt(lin[...], weights[pl.ds(h * HALF, HALF), :]).astype(BF16)
            for o in range(8):
                ig[o % 2, o // 2, h] = total[64 * o : 64 * o + 64]

    def pair_add():
        copies = pair_copies()
        sends = ring_copies()
        for n, block in enumerate((there, after, before, chip)):
            copies[n].wait_recv()
            for h in range(2):
                ig[core, block, h] = (
                    ig[core, block, h].astype(F32) + pair[block, h].astype(F32)
                ).astype(BF16)
            for m in ((0, 1), (2,), (3,), ())[n]:
                sends[m].start()

    def ring_second():
        copies = ring_copies()
        for n, block in ((0, after), (1, before)):
            copies[n].wait_recv()
            ig[core, block, n] = (
                ig[core, block, n].astype(F32) + xring[n].astype(F32)
            ).astype(BF16)
            copies[4 + n].start()

    def ring_last():
        copies = ring_copies()
        for n in (2, 3, 4, 5):
            copies[n].wait_recv()
        for h, first, second in ((0, 4, 3), (1, 2, 5)):
            ig_out[:, pl.ds(h * HALF, HALF)] = (
                ig[core, chip, h].astype(F32) + xring[first].astype(F32)
                + xring[second].astype(F32)
            ).astype(BF16)

    for copy in ring_kv[:3]:
        copy.start()
    load_og.wait()
    load_wo.wait()
    dattn[...] = nn(act[...], weights[:, : 2 * HD]).astype(BF16)
    for copy in load_w:
        copy.start()
    ring_kv[0].wait_recv()
    ring_kv[3].start()
    ring_kv[1].wait_recv()
    ring_kv[4].start()
    dkt[...] = jnp.zeros_like(dkt)
    dvt[...] = jnp.zeros_like(dvt)
    load_k.wait()
    load_v.wait()
    for copy in ring_kv[2:]:
        copy.wait_recv()
    lax.fori_loop(0, ROWS // TILE, forward, 0)
    multiply(0, attn[...])
    load_x.start()
    outer_first(0, order=(0, 1))
    outer_first(0, kinds=(0,), order=(2, 3))
    lax.fori_loop(0, ROWS // TILE, backward, 0)
    gout[0] = dkt[:, oldest].astype(BF16)
    gout[1] = dvt[:, oldest].astype(BF16)
    gout[2] = dvt[:, middle].astype(BF16)
    for copy in ring_back[:3]:
        copy.start()
    outer_first(0, kinds=(1,), order=(2, 3))
    load_x.wait()
    multiply(1, lin[:, : 2 * HD])
    outer_second(0, kinds=(0,))
    outer_first(1, kinds=(0,))
    ring_back[0].wait_recv()
    gin[0] = (gin[0].astype(F32) + dkt[:, middle]).astype(BF16)
    ring_back[3].start()
    ring_back[1].wait_recv()
    ring_back[4].start()
    outer_second(0, kinds=(1,))
    outer_first(1, kinds=(1,))
    for copy in load_w:
        copy.wait()
    for copy in ring_back[2:]:
        copy.wait_recv()
    key_grad = (dkt[:, latest] + gin[3].astype(F32)).T
    value_grad = (dvt[:, latest] + gin[2].astype(F32) + gin[4].astype(F32)).T
    lin[:, 2 * HD : 3 * HD] = rotate(key_grad, cos_ref[...], sin_ref[...]).astype(BF16)
    lin[:, 3 * HD :] = value_grad.astype(BF16)
    input_multiply()
    for copy in pair_copies():
        copy.start()
    multiply(2, lin[:, 2 * HD :])
    outer_first(2)
    pair_add()
    outer_second(1)
    inner_first(0)
    outer_second(2)
    ring_second()
    inner_second(0)
    inner_first(1)
    inner_second(1)
    inner_last(0)
    inner_first(2)
    inner_second(2)
    ring_last()
    inner_last(1)
    inner_last(2)
    for copy in ring_kv + ring_back:
        copy.wait_send()
    for r in range(3):
        for kind in range(2):
            for copy in outer(r, kind) + inner(r, kind):
                copy.wait_send()
    for copy in pair_copies() + ring_copies():
        copy.wait_send()


OUTS = (
    jax.ShapeDtypeStruct((64, D), BF16),
    jax.ShapeDtypeStruct((OWN, 2 * HD), F32),
    jax.ShapeDtypeStruct((OWN, HD), F32),
    jax.ShapeDtypeStruct((OWN, HD), F32),
    jax.ShapeDtypeStruct((OWN, 2 * HD), F32),
)


def fused(*operands):
    vmem = pl.BlockSpec(memory_space=pltpu.VMEM)
    anywhere = pl.BlockSpec(memory_space=pl.ANY)
    dma = pltpu.SemaphoreType.DMA
    return pl.pallas_call(
        fused_kernel,
        out_shape=OUTS,
        in_specs=[vmem] * 4 + [anywhere] * 8,
        out_specs=(vmem,) * 5,
        scratch_shapes=[
            pltpu.VMEM((BAND, HD), BF16),
            pltpu.VMEM((BAND, HD), BF16),
            pltpu.VMEM((ROWS, HD), BF16),
            pltpu.VMEM((ROWS, D), BF16),
            pltpu.VMEM((D, 4 * HD), BF16),
            pltpu.VMEM((ROWS, 2 * HD), BF16),
            pltpu.VMEM((ROWS, 2 * HD), BF16),
            pltpu.VMEM((ROWS, 4 * HD), BF16),
            pltpu.VMEM((ROWS // TILE, 2 * TILE, WINDOW), F32),
            pltpu.VMEM((HD, BAND), F32),
            pltpu.VMEM((HD, BAND), F32),
            pltpu.VMEM((3, HD, ROWS), BF16),
            pltpu.VMEM((5, HD, ROWS), BF16),
            pltpu.VMEM((3, 2, 16, OWN, HD), BF16),
            pltpu.VMEM((3, 2, 4, OWN, HD), BF16),
            pltpu.VMEM((3, 2, 6, 2, OWN, HD), BF16),
            pltpu.VMEM((3, 2, 6, TOP, HD), BF16),
            pltpu.VMEM((2, 4, 2, 64, HALF), BF16),
            pltpu.VMEM((4, 2, 64, HALF), BF16),
            pltpu.VMEM((6, 64, HALF), BF16),
            dma((8,)),
            dma((5,)), dma((5,)), dma((5,)), dma((5,)),
            dma((3, 2, 6)), dma((3, 2, 6)), dma((3, 2, 6)), dma((3, 2, 6)),
            dma((4,)), dma((4,)), dma((6,)), dma((6,)),
        ],
        compiler_params=pltpu.CompilerParams(
            collective_id=0, has_side_effects=True, vmem_limit_bytes=66_900_000
        ),
        name="fused",
    )(*operands)


def finish_kernel(*refs):
    for src, dst in zip(refs[:5], refs[5:]):
        dst[...] = src[...]


def finish(*results):
    vmem = pl.BlockSpec(memory_space=pltpu.VMEM)
    return pl.pallas_call(
        finish_kernel, out_shape=OUTS, in_specs=[vmem] * 5, out_specs=(vmem,) * 5,
        compiler_params=pltpu.CompilerParams(vmem_limit_bytes=8 << 20),
        name="finish",
    )(*results)


def on_device(
    inputs, queries, key_states, value_states, out_grad, positions,
    w_query, w_key, w_value, w_output,
):
    block = lax.axis_index("context")
    row = jnp.arange(ROWS, dtype=jnp.int32)
    index = block * ROWS + row
    low = jnp.maximum(jnp.maximum(index - (W - 1), index - positions), 0) - (block - 2) * ROWS
    order = jnp.arange(HD // 2, dtype=F32)
    freq = jnp.power(F32(10000.0), order * (-2.0 / HD))
    angle = positions.astype(F32)[:, None] * freq[None, :]
    cosine, sine = jnp.cos(angle), jnp.sin(angle)
    cosine = jnp.concatenate([cosine, cosine], axis=1)
    sine = jnp.concatenate([sine, -sine], axis=1)
    return finish(
        *fused(
            queries, low[:, None], cosine, sine, key_states, value_states,
            inputs, out_grad, w_query, w_key, w_value, w_output,
        )
    )


def solution(mesh):
    rows = ("dp", "context")
    return jax.shard_map(
        on_device,
        mesh=mesh,
        in_specs=(
            P(rows, None), P(rows, "tensor"), P(rows, "tensor"), P(rows, "tensor"),
            P(rows, None), P(rows), P(None, "tensor"), P(None, "tensor"),
            P(None, "tensor"), P(None, "tensor"),
        ),
        out_specs=(
            P(("dp", "context", "tensor"), None), P(rows, "tensor"), P(rows, "tensor"),
            P(rows, "tensor"), P(rows, "tensor"),
        ),
        check_vma=False,
    )
```

```python
import functools

import jax
import jax.numpy as jnp
import numpy as np
from jax import lax
from jax.experimental import pallas as pl
from jax.experimental.pallas import tpu as pltpu
from jax.sharding import PartitionSpec as P

HD = 128
W = 1024
QSCALAR = 168
D = 5376
ROWS = 512
TILE = 128
WINDOW = W + TILE
BAND = 3 * ROWS
OWN = D // 16
HALF = D // 2
SPAN = 1408
TOP = 176
F32 = jnp.float32
BF16 = jnp.bfloat16
MESH = pl.DeviceIdType.MESH


def nt(left, right):
    return lax.dot_general(left, right, (((1,), (1,)), ((), ())), preferred_element_type=F32)


def nn(left, right):
    return jnp.dot(left, right, preferred_element_type=F32)


def rotate(grad, cosine, sine):
    return grad * cosine + pltpu.roll(grad, HD // 2, 1) * sine


def step(axis, index, delta):
    size = 4
    return {axis: lax.rem(index + delta + size, size)}


def fused_kernel(
    q_ref, k_ref, v_ref, place_ref, freq_ref,
    x_hbm, og_hbm, wq_hbm, wk_hbm, wv_hbm, wo_hbm,
    ig_hbm, gq_hbm, gk_hbm, gv_hbm, go_hbm,
    ig_out, gq_out, gk_out, gv_out, go_out, low_ref, cos_ref, sin_ref,
    keys, values, relay, og, wide_x, wq, wkv, dattn, attn, lin, swap_out, swap_in,
    probs, dkt, dvt, gout, gin, product,
    parts, near, mid_half, mid_full, far_half, far_full, ig, pair, xring, load_sem, out_sem,
    a_send, a_recv, b_send, b_recv, c_send, c_recv, e_send, e_recv,
    f_send, f_recv, g_send, g_recv, h_send, h_recv, l_send, l_recv,
):
    scale = QSCALAR ** (-0.5)
    z = lax.axis_index("dp")
    y = lax.axis_index("context")
    t = lax.axis_index("tensor")
    core = lax.rem(t, 2)
    chip = t // 2
    partner = {"tensor": t + 1 - 2 * core}
    tplus, tminus, tfar = lax.rem(t + 2, 8), lax.rem(t + 6, 8), lax.rem(t + 4, 8)
    xplus, xminus = {"tensor": tplus}, {"tensor": tminus}
    yplus, yminus = step("context", y, 1), step("context", y, -1)
    zplus, zminus, zfar = step("dp", z, 1), step("dp", z, -1), step("dp", z, 2)
    oldest, middle, latest = pl.ds(0, ROWS), pl.ds(ROWS, ROWS), pl.ds(2 * ROWS, ROWS)

    def load(n, src, dst):
        return pltpu.make_async_copy(src, dst, load_sem.at[n])

    def columns(delta):
        there = lax.rem(z + delta, 4)
        return pl.ds(pl.multiple_of(4 * OWN * there - 64 * lax.rem(there, 2), 128), SPAN)

    load_og = load(0, og_hbm, og)
    load_wo = load(1, wo_hbm, wq)
    load_x = load(4, x_hbm.at[:, columns(0)], wide_x.at[0])
    load_wq = load(5, wq_hbm, wq)
    load_wk = load(6, wk_hbm, wkv.at[:, pl.ds(0, HD)])
    load_wv = load(7, wv_hbm, wkv.at[:, pl.ds(HD, HD)])
    barrier = pltpu.get_barrier_semaphore()
    for device in (yplus, yminus, zplus, zminus, zfar, xplus, xminus, partner):
        pl.semaphore_signal(barrier, inc=1, device_id=device, device_id_type=MESH)
    pl.semaphore_wait(barrier, 8)

    lines = (("dp", z, "context", y), ("context", y, "dp", z))

    def remote(src, dst, send, recv, device):
        return pltpu.make_async_remote_copy(
            src_ref=src, dst_ref=dst, send_sem=send, recv_sem=recv,
            device_id=device, device_id_type=MESH,
        )

    def ring(n, src, dst, device):
        return remote(src, dst, a_send.at[n], a_recv.at[n], device)

    ring_kv = (
        ring(0, k_ref, keys.at[middle], yplus),
        ring(1, v_ref, relay, yminus),
        ring(2, v_ref, values.at[middle], yplus),
        ring(3, keys.at[middle], keys.at[oldest], yplus),
        ring(4, relay, values.at[oldest], yminus),
    )

    def back(n, src, dst, device):
        return remote(gout.at[src] if src < 3 else gin.at[src - 3], gin.at[dst],
                      b_send.at[n], b_recv.at[n], device)

    ring_back = (
        back(0, 0, 0, yminus), back(1, 1, 1, yplus), back(2, 2, 2, yminus),
        back(3, 3, 3, yminus), back(4, 4, 4, yplus),
    )

    def eighth(where, start=0, size=64):
        return wide_x.at[pl.ds(1, 3), pl.ds(pl.multiple_of(64 * where + start, 16), size)]

    def move(n, src, dst, device):
        return remote(src, dst, h_send.at[n], h_recv.at[n], device)

    mine = pl.ds(pl.multiple_of(64 * t, 64), 64)
    move_z = [
        move(n, x_hbm.at[mine, columns(delta)], wide_x.at[4 - delta, mine], device)
        for n, (delta, device) in enumerate(((1, zplus), (3, zminus), (2, zfar)))
    ]
    move_x = [
        move(3, eighth(t), eighth(t), xplus),
        move(4, eighth(t), eighth(t), xminus),
        move(5, eighth(tminus, 0, 32), eighth(tminus, 0, 32), xplus),
        move(6, eighth(tplus, 32, 32), eighth(tplus, 32, 32), xminus),
    ]
    move_core = [
        move(7 + n, eighth(where), eighth(where), partner)
        for n, where in enumerate((t, tminus, tplus, tfar))
    ]
    move_w = [
        move(11, wk_hbm, wkv.at[:, pl.ds(2 * HD, HD)], partner),
        move(12, wv_hbm, wkv.at[:, pl.ds(3 * HD, HD)], partner),
    ]
    move_swap = move(13, swap_out, swap_in, partner)

    @functools.cache
    def gather(r):
        first, second = pl.ds(0, ROWS // 2), pl.ds(ROWS // 2, ROWS // 2)
        plan = (
            (lin.at[r, 0], lin.at[r, 3], zplus),
            (lin.at[r, 0], lin.at[r, 1], zminus),
            (lin.at[r, 3, first], lin.at[r, 2, first], zplus),
            (lin.at[r, 1, second], lin.at[r, 2, second], zminus),
        )
        return [
            remote(src, dst, l_send.at[r, n], l_recv.at[r, n], device)
            for n, (src, dst, device) in enumerate(plan)
        ]

    def gather_relay(r):
        for n in range(2):
            gather(r)[n].wait_recv()
            gather(r)[2 + n].start()

    @functools.cache
    def outer(kind):
        axis, me, _, _ = lines[kind]
        there = 4 * lax.rem(me + 2, 4)
        after = 4 * lax.rem(me + 1, 4)
        before = 4 * lax.rem(me + 3, 4)
        up, down = step(axis, me, 1), step(axis, me, -1)
        plan = (
            (there, up), (there + 2, down), (after + 2, up), (before, down),
            (after, up), (before + 2, down),
        )
        return [
            remote(
                parts.at[kind, pl.ds(start, 2)], near.at[kind, n],
                c_send.at[kind, n], c_recv.at[kind, n], device,
            )
            for n, (start, device) in enumerate(plan)
        ]

    upper, lower = pl.ds(0, TOP), pl.ds(TOP, OWN - TOP)
    stages = (
        ("context", y, mid_half.at[0], far_half.at[0]),
        ("dp", z, mid_half.at[1], far_half.at[1]),
        ("context", y, mid_full.at[0], far_full.at[0]),
        ("context", y, mid_full.at[1], far_full.at[1]),
    )

    @functools.cache
    def inner(s):
        axis, me, mid, far = stages[s]
        there = lax.rem(me + 2, 4)
        after = lax.rem(me + 1, 4)
        before = lax.rem(me + 3, 4)
        up, down = step(axis, me, 1), step(axis, me, -1)
        plan = (
            (there, upper, up), (there, lower, down), (after, lower, up), (before, upper, down),
            (after, upper, up), (before, lower, down),
        )
        return [
            remote(
                mid.at[block, rows], far.at[n, pl.ds(0, rows.size)],
                e_send.at[s, n], e_recv.at[s, n], device,
            )
            for n, (block, rows, device) in enumerate(plan)
        ]

    def stacked(ref, rows):
        return jnp.concatenate([ref[rows, :HD], ref[rows, HD:]], axis=0)

    def forward(i, carry):
        base = pl.multiple_of(i * TILE, TILE)
        rows = pl.ds(base, TILE)
        wide = pl.ds(base, WINDOW)
        low = low_ref[rows, :1] - base
        low = jnp.concatenate([low, low], axis=0)
        row = lax.broadcasted_iota(jnp.int32, (2 * TILE, 1), 0) % TILE
        col = lax.broadcasted_iota(jnp.int32, (2 * TILE, WINDOW), 1)
        allowed = (col >= low) & (col <= row + W)
        scores = jnp.where(allowed, nt(stacked(q_ref, rows), keys[wide, :]) * scale, -1e30)
        top = jnp.max(scores, axis=-1, keepdims=True)
        raised = jnp.exp(scores - top)
        prob = raised / jnp.sum(raised, axis=-1, keepdims=True)
        probs[i] = prob
        result = nn(prob.astype(BF16), values[wide, :]).astype(BF16)
        attn[rows, :HD] = result[:TILE]
        attn[rows, HD:] = result[TILE:]
        return carry

    def backward(i, carry):
        base = pl.multiple_of(i * TILE, TILE)
        rows = pl.ds(base, TILE)
        wide = pl.ds(base, WINDOW)
        grad = stacked(dattn, rows)
        prob = probs[i]
        dprobs = nt(grad, values[wide, :])
        delta = jnp.sum(
            grad.astype(F32) * stacked(attn, rows).astype(F32), axis=-1, keepdims=True
        )
        dscores = (prob * (dprobs - delta) * scale).astype(BF16)
        dq = nn(dscores, keys[wide, :])
        lin[0, 0, rows, :HD] = rotate(dq[:TILE], cos_ref[rows, :], sin_ref[rows, :]).astype(BF16)
        lin[0, 0, rows, HD:] = rotate(
            dq[TILE:], cos_ref[rows, :], sin_ref[rows, :]
        ).astype(BF16)
        dkt[:, wide] += nn(stacked(q_ref, rows).T, dscores)
        dvt[:, wide] += nn(grad.T, prob.astype(BF16))
        return carry

    def outer_multiply():
        right = attn[...]

        def body(i, carry):
            lanes = pl.ds(pl.multiple_of(i * HALF, 128), HALF)
            result = lax.dot_general(
                og[:, lanes], right, (((0,), (0,)), ((), ())), preferred_element_type=F32
            ).astype(BF16)
            for j in range(8):
                rows = slice(OWN * j, OWN * j + OWN)
                parts[0, 8 * i + j] = result[rows, :HD]
                parts[1, 4 * (j % 4) + 2 * i + j // 4] = result[rows, HD:]
            return carry

        lax.fori_loop(0, 2, body, 0)

    def outer_first(kinds, order):
        for n in order:
            for kind in kinds:
                outer(kind)[n].start()

    def outer_second(kind):
        me = lines[kind][1]
        after = 4 * lax.rem(me + 1, 4)
        before = 4 * lax.rem(me + 3, 4)
        for n, start in ((0, after), (1, before + 2)):
            outer(kind)[n].wait_recv()
            where = pl.ds(start, 2)
            parts[kind, where] = (
                parts[kind, where].astype(F32) + near[kind, n].astype(F32)
            ).astype(BF16)
            outer(kind)[4 + n].start()

    def inner_start(s):
        for n in range(4):
            inner(s)[n].start()

    def outer_last(kind):
        me = lines[kind][1]
        for n in (2, 3, 4, 5):
            outer(kind)[n].wait_recv()
        for block in range(4):
            first, second = (4, 3) if block < 2 else (2, 5)
            mid_half[kind, block] = (
                parts[kind, 4 * me + block].astype(F32)
                + near[kind, first, block % 2].astype(F32)
                + near[kind, second, block % 2].astype(F32)
            ).astype(BF16)
        inner_start(kind)

    def inner_multiply(r):
        product[...] = jnp.zeros_like(product)

        def body(j, carry):
            product[...] += lax.dot_general(
                wide_x[j], lin[r, j], (((0,), (0,)), ((), ())), preferred_element_type=F32
            )
            return carry

        lax.fori_loop(0, 4, body, 0)
        for block in range(4):
            start = pl.multiple_of(64 * lax.rem(z, 2) + OWN * block, 16)
            mid_full[r, block] = product[pl.ds(start, OWN), :].astype(BF16)
        inner_start(2 + r)

    def inner_second(s):
        _, me, mid, far = stages[s]
        after = lax.rem(me + 1, 4)
        before = lax.rem(me + 3, 4)
        for n, block, rows in ((0, after, upper), (1, before, lower)):
            inner(s)[n].wait_recv()
            mid[block, rows] = (
                mid[block, rows].astype(F32) + far[n, pl.ds(0, rows.size)].astype(F32)
            ).astype(BF16)
            inner(s)[4 + n].start()

    def inner_last(s, outs):
        _, me, mid, far = stages[s]
        for n in (2, 3, 4, 5):
            inner(s)[n].wait_recv()
        for rows, first, second in ((upper, 4, 3), (lower, 2, 5)):
            size = pl.ds(0, rows.size)
            total = (
                mid[me, rows].astype(F32) + far[first, size].astype(F32)
                + far[second, size].astype(F32)
            )
            for out, source, lanes in outs:
                out[rows, lanes] = total[:, source]

    there, after, before = lax.rem(chip + 2, 4), lax.rem(chip + 1, 4), lax.rem(chip + 3, 4)
    pair_copies = [
        remote(ig.at[1 - core, block], pair.at[block], f_send.at[n], f_recv.at[n], partner)
        for n, block in enumerate((there, after, before, chip))
    ]
    ring_x = [
        remote(ig.at[core, block, h], xring.at[n], g_send.at[n], g_recv.at[n], device)
        for n, (block, h, device) in enumerate((
            (there, 0, xplus), (there, 1, xminus), (after, 1, xplus), (before, 0, xminus),
            (after, 0, xplus), (before, 1, xminus),
        ))
    ]

    def query_multiply():
        for h in range(2):
            total = nt(lin[0, 0], wq[pl.ds(h * HALF, HALF), :]).astype(BF16)
            for o in range(8):
                ig[o % 2, o // 2, h] = total[64 * o : 64 * o + 64]

    def core_rows(which):
        return [
            lin[1, 0, pl.ds(pl.multiple_of(64 * (2 * n + which), 64), 64), :] for n in range(4)
        ]

    def key_multiply():
        left = jnp.concatenate(core_rows(core), axis=0)
        left = jnp.concatenate([left, swap_in[...]], axis=1)
        for n in range(4):
            pair_copies[n].wait_recv()
        for h in range(2):
            total = nt(left, wkv[pl.ds(h * HALF, HALF), :])
            for n in range(4):
                ig[core, n, h] = (
                    total[64 * n : 64 * n + 64] + ig[core, n, h].astype(F32)
                    + pair[n, h].astype(F32)
                ).astype(BF16)
            for n in ((0, 3), (1, 2))[h]:
                ring_x[n].start()

    def ring_second():
        for n, block in ((0, after), (1, before)):
            ring_x[n].wait_recv()
            ig[core, block, n] = (
                ig[core, block, n].astype(F32) + xring[n].astype(F32)
            ).astype(BF16)
            ring_x[4 + n].start()

    def ring_last():
        for n in (2, 3, 4, 5):
            ring_x[n].wait_recv()
        for h, first, second in ((0, 4, 3), (1, 2, 5)):
            ig_out[:, pl.ds(h * HALF, HALF)] = (
                ig[core, chip, h].astype(F32) + xring[first].astype(F32)
                + xring[second].astype(F32)
            ).astype(BF16)

    def store(n, src, dst):
        return pltpu.make_async_copy(src, dst, out_sem.at[n])

    store_ig = store(0, ig_out, ig_hbm)
    store_gq = store(1, gq_out, gq_hbm)
    store_gk = store(2, gk_out, gk_hbm)
    store_gv = store(3, gv_out, gv_hbm)
    store_go = store(4, go_out, go_hbm)

    for copy in ring_kv[:3] + (load_og, load_wo) + tuple(move_z):
        copy.start()
    for copy in (load_x, load_wk, load_wv) + tuple(move_w):
        copy.start()
    keys[latest, :] = k_ref[...]
    values[latest, :] = v_ref[...]
    lane = lax.broadcasted_iota(jnp.int32, (TILE, HD), 1)
    for n in range(ROWS // TILE):
        rows = slice(TILE * n, TILE * n + TILE)
        place = jnp.broadcast_to(place_ref[n : n + 1, :].astype(F32), (TILE, HD)).T
        angle = place * freq_ref[...]
        cos_ref[rows, :] = jnp.cos(angle)
        sine = jnp.sin(angle)
        sin_ref[rows, :] = jnp.where(lane < HD // 2, sine, -sine)
        row = lax.broadcasted_iota(jnp.int32, (TILE, HD), 0) + TILE * n
        reach = jnp.minimum(place.astype(jnp.int32), W - 1)
        low_ref[rows, :] = jnp.maximum(row - reach + 2 * ROWS, (2 - y) * ROWS)
    dkt[...] = jnp.zeros_like(dkt)
    dvt[...] = jnp.zeros_like(dvt)
    for n in range(2):
        ring_kv[n].wait_recv()
        ring_kv[3 + n].start()
    load_og.wait()
    load_wo.wait()
    dattn[...] = nn(og[...], wq[...]).astype(BF16)
    load_wq.start()
    for copy in move_z:
        copy.wait_recv()
    for copy in move_x[:2] + move_core[:1]:
        copy.start()
    for copy in ring_kv[2:]:
        copy.wait_recv()
    lax.fori_loop(0, ROWS // TILE, forward, 0)
    outer_multiply()
    outer_first((0, 1), (0, 1))
    outer_first((0,), (2, 3))
    lax.fori_loop(0, ROWS // TILE, backward, 0)
    gout[0] = dkt[:, oldest].astype(BF16)
    gout[1] = dvt[:, oldest].astype(BF16)
    gout[2] = dvt[:, middle].astype(BF16)
    for copy in ring_back[:3] + tuple(gather(0)[:2]):
        copy.start()
    load_wq.wait()
    query_multiply()
    for copy in pair_copies:
        copy.start()
    ring_back[0].wait_recv()
    gin[0] = (gin[0].astype(F32) + dkt[:, middle]).astype(BF16)
    ring_back[3].start()
    ring_back[1].wait_recv()
    ring_back[4].start()
    outer_first((1,), (2, 3))
    outer_second(0)
    for n in range(2):
        move_x[n].wait_recv()
        move_x[2 + n].start()
        move_core[1 + n].start()
    outer_second(1)
    for copy in ring_back[2:]:
        copy.wait_recv()
    key_grad = (dkt[:, latest] + gin[3].astype(F32)).T
    value_grad = (dvt[:, latest] + gin[2].astype(F32) + gin[4].astype(F32)).T
    lin[1, 0, :, :HD] = rotate(key_grad, cos_ref[...], sin_ref[...]).astype(BF16)
    lin[1, 0, :, HD:] = value_grad.astype(BF16)
    swap_out[...] = jnp.concatenate(core_rows(1 - core), axis=0)
    move_swap.start()
    for copy in gather(1)[:2]:
        copy.start()
    load_wk.wait()
    load_wv.wait()
    for copy in move_w:
        copy.wait_recv()
    move_swap.wait_recv()
    key_multiply()
    gather_relay(0)
    for copy in move_x[2:]:
        copy.wait_recv()
    move_core[3].start()
    outer_last(0)
    outer_last(1)
    load_x.wait()
    for copy in move_core + gather(0)[2:]:
        copy.wait_recv()
    inner_multiply(0)
    gather_relay(1)
    inner_second(0)
    inner_second(1)
    ring_second()
    inner_second(2)
    for copy in gather(1)[2:]:
        copy.wait_recv()
    inner_multiply(1)
    every = slice(0, 2 * HD)
    left, right = slice(0, HD), slice(HD, 2 * HD)
    inner_last(0, ((go_out, left, left),))
    inner_last(1, ((go_out, left, right),))
    store_go.start()
    inner_second(3)
    inner_last(2, ((gq_out, every, every),))
    store_gq.start()
    inner_last(3, ((gk_out, left, left), (gv_out, right, left)))
    store_gk.start()
    store_gv.start()
    ring_last()
    store_ig.start()
    for copy in (store_go, store_gq, store_gk, store_gv, store_ig):
        copy.wait()
    sent = list(ring_kv + ring_back) + move_z + move_x + move_core + move_w + [move_swap]
    sent += pair_copies + ring_x
    for s in range(4):
        sent += inner(s)
    for n in range(2):
        sent += gather(n) + outer(n)
    for copy in sent:
        copy.wait_send()


OUTS = (
    jax.ShapeDtypeStruct((64, D), BF16),
    jax.ShapeDtypeStruct((OWN, 2 * HD), F32),
    jax.ShapeDtypeStruct((OWN, HD), F32),
    jax.ShapeDtypeStruct((OWN, HD), F32),
    jax.ShapeDtypeStruct((OWN, 2 * HD), F32),
)


def fused(*operands):
    vmem = pl.BlockSpec(memory_space=pltpu.VMEM)
    anywhere = pl.BlockSpec(memory_space=pl.ANY)
    dma = pltpu.SemaphoreType.DMA
    buffers = (
        ((ROWS, HD), jnp.int32),
        ((ROWS, HD), F32),
        ((ROWS, HD), F32),
        ((BAND, HD), BF16),
        ((BAND, HD), BF16),
        ((ROWS, HD), BF16),
        ((ROWS, D), BF16),
        ((4, ROWS, SPAN), BF16),
        ((D, 2 * HD), BF16),
        ((D, 4 * HD), BF16),
        ((ROWS, 2 * HD), BF16),
        ((ROWS, 2 * HD), BF16),
        ((2, 4, ROWS, 2 * HD), BF16),
        ((ROWS // 2, 2 * HD), BF16),
        ((ROWS // 2, 2 * HD), BF16),
        ((ROWS // TILE, 2 * TILE, WINDOW), F32),
        ((HD, BAND), F32),
        ((HD, BAND), F32),
        ((3, HD, ROWS), BF16),
        ((5, HD, ROWS), BF16),
        ((SPAN, 2 * HD), F32),
        ((2, 16, OWN, HD), BF16),
        ((2, 6, 2, OWN, HD), BF16),
        ((2, 4, OWN, HD), BF16),
        ((2, 4, OWN, 2 * HD), BF16),
        ((2, 6, TOP, HD), BF16),
        ((2, 6, TOP, 2 * HD), BF16),
        ((2, 4, 2, 64, HALF), BF16),
        ((4, 2, 64, HALF), BF16),
        ((6, 64, HALF), BF16),
    )
    counts = ((5,), (5,), (2, 6), (4, 6), (4,), (6,), (14,), (2, 4))
    return pl.pallas_call(
        fused_kernel,
        out_shape=OUTS,
        in_specs=[vmem] * 5 + [anywhere] * 6,
        out_specs=(anywhere,) * 5,
        scratch_shapes=[pltpu.VMEM(out.shape, out.dtype) for out in OUTS]
        + [pltpu.VMEM(*buffer) for buffer in buffers]
        + [dma((8,)), dma((5,))]
        + [dma(count) for count in counts for _ in range(2)],
        compiler_params=pltpu.CompilerParams(
            collective_id=0, has_side_effects=True, vmem_limit_bytes=66_900_000
        ),
        name="fused",
    )(*operands)


def finish_kernel(*refs):
    sources, targets, buffers, sems = refs[:5], refs[5:10], refs[10:15], refs[15]
    order = (0, 1, 4, 2, 3)
    loads = [pltpu.make_async_copy(sources[n], buffers[n], sems.at[0, n]) for n in range(5)]
    stores = [pltpu.make_async_copy(buffers[n], targets[n], sems.at[1, n]) for n in range(5)]
    for n in order:
        loads[n].start()
    for n in order:
        loads[n].wait()
        stores[n].start()
    for n in order:
        stores[n].wait()


def finish(*results):
    anywhere = pl.BlockSpec(memory_space=pl.ANY)
    return pl.pallas_call(
        finish_kernel, out_shape=OUTS, in_specs=[anywhere] * 5, out_specs=(anywhere,) * 5,
        scratch_shapes=[pltpu.VMEM(out.shape, out.dtype) for out in OUTS]
        + [pltpu.SemaphoreType.DMA((2, 5))],
        compiler_params=pltpu.CompilerParams(vmem_limit_bytes=66_900_000),
        name="finish",
    )(*results)


def on_device(
    inputs, queries, key_states, value_states, out_grad, positions,
    w_query, w_key, w_value, w_output,
):
    index = np.arange(HD) % (HD // 2)
    freq = jnp.asarray((10000.0 ** (index * (-2.0 / HD))).astype(np.float32)[None, :])
    return finish(
        *fused(
            queries, key_states, value_states, positions.reshape(ROWS // TILE, TILE), freq,
            inputs, out_grad, w_query, w_key, w_value, w_output,
        )
    )


def solution(mesh):
    rows = ("dp", "context")
    return jax.shard_map(
        on_device,
        mesh=mesh,
        in_specs=(
            P(rows, None), P(rows, "tensor"), P(rows, "tensor"), P(rows, "tensor"),
            P(rows, None), P(rows), P(None, "tensor"), P(None, "tensor"),
            P(None, "tensor"), P(None, "tensor"),
        ),
        out_specs=(
            P(("dp", "context", "tensor"), None), P(rows, "tensor"), P(rows, "tensor"),
            P(rows, "tensor"), P(rows, "tensor"),
        ),
        check_vma=False,
    )
```

```python
import functools

import jax
import jax.numpy as jnp
import numpy as np
from jax import lax
from jax.experimental import pallas as pl
from jax.experimental.pallas import tpu as pltpu
from jax.sharding import PartitionSpec as P

HD = 128
W = 1024
QSCALAR = 168
D = 5376
ROWS = 512
TILE = 128
WINDOW = W + TILE
BAND = 3 * ROWS
OWN = D // 16
HALF = D // 2
SPAN = 1408
TOP = 176
LOG2E = 1.4426950408889634
F32 = jnp.float32
BF16 = jnp.bfloat16
MESH = pl.DeviceIdType.MESH


def nt(left, right):
    return lax.dot_general(left, right, (((1,), (1,)), ((), ())), preferred_element_type=F32)


def nn(left, right):
    return jnp.dot(left, right, preferred_element_type=F32)


def rotate(grad, cosine, sine):
    return grad * cosine + pltpu.roll(grad, HD // 2, 1) * sine


def step(axis, index, delta):
    size = 4
    return {axis: lax.rem(index + delta + size, size)}


def fused_kernel(
    q_hbm, k_hbm, v_hbm, place_hbm, freq_hbm,
    x_hbm, og_hbm, wq_hbm, wk_hbm, wv_hbm, wo_hbm,
    ig_hbm, gq_hbm, gk_hbm, gv_hbm, go_hbm,
    ig_out, gq_out, gk_out, gv_out, go_out, low_ref, cos_ref, sin_ref,
    q_ref, place_ref, freq_ref, keys, values, relay, og, wide_x, wq, wkv, dattn, attn, lin, swap_out, swap_in,
    probs, dkt, dvt, gout, gin, product,
    parts, near, mid_half, mid_full, far_half, far_full, ig, pair, xring, load_sem, out_sem,
    a_send, a_recv, b_send, b_recv, c_send, c_recv, e_send, e_recv,
    f_send, f_recv, g_send, g_recv, h_send, h_recv, l_send, l_recv,
):
    scale = QSCALAR ** (-0.5)
    z = lax.axis_index("dp")
    y = lax.axis_index("context")
    t = lax.axis_index("tensor")
    core = lax.rem(t, 2)
    chip = t // 2
    partner = {"tensor": t + 1 - 2 * core}
    tplus, tminus, tfar = lax.rem(t + 2, 8), lax.rem(t + 6, 8), lax.rem(t + 4, 8)
    xplus, xminus = {"tensor": tplus}, {"tensor": tminus}
    yplus, yminus = step("context", y, 1), step("context", y, -1)
    zplus, zminus, zfar = step("dp", z, 1), step("dp", z, -1), step("dp", z, 2)
    oldest, middle, latest = pl.ds(0, ROWS), pl.ds(ROWS, ROWS), pl.ds(2 * ROWS, ROWS)

    def load(n, src, dst):
        return pltpu.make_async_copy(src, dst, load_sem.at[n])

    def columns(delta):
        there = lax.rem(z + delta, 4)
        return pl.ds(pl.multiple_of(4 * OWN * there - 64 * lax.rem(there, 2), 128), SPAN)

    load_og = load(0, og_hbm, og)
    load_wo = load(1, wo_hbm, wq)
    load_x = load(4, x_hbm.at[:, columns(0)], wide_x.at[0])
    load_wq = load(5, wq_hbm, wq)
    load_wk = load(6, wk_hbm, wkv.at[:, pl.ds(0, HD)])
    load_wv = load(7, wv_hbm, wkv.at[:, pl.ds(HD, HD)])
    small = [
        load(8 + n, src, dst)
        for n, (src, dst) in enumerate((
            (place_hbm, place_ref), (freq_hbm, freq_ref), (q_hbm, q_ref),
            (k_hbm, keys.at[latest]), (v_hbm, values.at[latest]),
        ))
    ]
    barrier = pltpu.get_barrier_semaphore()
    for device in (zfar, yplus, yminus, zplus, zminus, xplus, xminus, partner):
        pl.semaphore_signal(barrier, inc=1, device_id=device, device_id_type=MESH)
    for copy in small:
        copy.start()
    pl.semaphore_wait(barrier, 8)

    lines = (("dp", z, "context", y), ("context", y, "dp", z))

    def remote(src, dst, send, recv, device):
        return pltpu.make_async_remote_copy(
            src_ref=src, dst_ref=dst, send_sem=send, recv_sem=recv,
            device_id=device, device_id_type=MESH,
        )

    def ring(n, src, dst, device):
        return remote(src, dst, a_send.at[n], a_recv.at[n], device)

    ring_kv = (
        ring(0, k_hbm, keys.at[middle], yplus),
        ring(1, v_hbm, relay, yminus),
        ring(2, v_hbm, values.at[middle], yplus),
        ring(3, keys.at[middle], keys.at[oldest], yplus),
        ring(4, relay, values.at[oldest], yminus),
    )

    def back(n, src, dst, device):
        return remote(gout.at[src] if src < 3 else gin.at[src - 3], gin.at[dst],
                      b_send.at[n], b_recv.at[n], device)

    ring_back = (
        back(0, 0, 0, yminus), back(1, 1, 1, yplus), back(2, 2, 2, yminus),
        back(3, 3, 3, yminus), back(4, 4, 4, yplus),
    )

    def eighth(where, start=0, size=64):
        return wide_x.at[pl.ds(1, 3), pl.ds(pl.multiple_of(64 * where + start, 16), size)]

    def move(n, src, dst, device):
        return remote(src, dst, h_send.at[n], h_recv.at[n], device)

    mine = pl.ds(pl.multiple_of(64 * t, 64), 64)
    move_z = [
        move(n, x_hbm.at[mine, columns(delta)], wide_x.at[4 - delta, mine], device)
        for n, (delta, device) in enumerate(((1, zplus), (3, zminus), (2, zfar)))
    ]
    move_x = [
        move(3, eighth(t), eighth(t), xplus),
        move(4, eighth(t), eighth(t), xminus),
        move(5, eighth(tminus, 0, 32), eighth(tminus, 0, 32), xplus),
        move(6, eighth(tplus, 32, 32), eighth(tplus, 32, 32), xminus),
    ]
    move_core = [
        move(7 + n, eighth(where), eighth(where), partner)
        for n, where in enumerate((t, tminus, tplus, tfar))
    ]
    move_w = [
        move(11, wk_hbm, wkv.at[:, pl.ds(2 * HD, HD)], partner),
        move(12, wv_hbm, wkv.at[:, pl.ds(3 * HD, HD)], partner),
    ]
    move_swap = move(13, swap_out, swap_in, partner)

    @functools.cache
    def gather(r):
        first, second = pl.ds(0, ROWS // 2), pl.ds(ROWS // 2, ROWS // 2)
        plan = (
            (lin.at[r, 0], lin.at[r, 3], zplus),
            (lin.at[r, 0], lin.at[r, 1], zminus),
            (lin.at[r, 3, first], lin.at[r, 2, first], zplus),
            (lin.at[r, 1, second], lin.at[r, 2, second], zminus),
        )
        return [
            remote(src, dst, l_send.at[r, n], l_recv.at[r, n], device)
            for n, (src, dst, device) in enumerate(plan)
        ]

    def gather_relay(r):
        for n in range(2):
            gather(r)[n].wait_recv()
            gather(r)[2 + n].start()

    @functools.cache
    def outer(kind):
        axis, me, _, _ = lines[kind]
        there = 4 * lax.rem(me + 2, 4)
        after = 4 * lax.rem(me + 1, 4)
        before = 4 * lax.rem(me + 3, 4)
        up, down = step(axis, me, 1), step(axis, me, -1)
        plan = (
            (there, up), (there + 2, down), (after + 2, up), (before, down),
            (after, up), (before + 2, down),
        )
        return [
            remote(
                parts.at[kind, pl.ds(start, 2)], near.at[kind, n],
                c_send.at[kind, n], c_recv.at[kind, n], device,
            )
            for n, (start, device) in enumerate(plan)
        ]

    upper, lower = pl.ds(0, TOP), pl.ds(TOP, OWN - TOP)
    stages = (
        ("context", y, mid_half.at[0], far_half.at[0]),
        ("dp", z, mid_half.at[1], far_half.at[1]),
        ("context", y, mid_full.at[0], far_full.at[0]),
        ("context", y, mid_full.at[1], far_full.at[1]),
    )

    @functools.cache
    def inner(s):
        axis, me, mid, far = stages[s]
        there = lax.rem(me + 2, 4)
        after = lax.rem(me + 1, 4)
        before = lax.rem(me + 3, 4)
        up, down = step(axis, me, 1), step(axis, me, -1)
        plan = (
            (there, upper, up), (there, lower, down), (after, lower, up), (before, upper, down),
            (after, upper, up), (before, lower, down),
        )
        return [
            remote(
                mid.at[block, rows], far.at[n, pl.ds(0, rows.size)],
                e_send.at[s, n], e_recv.at[s, n], device,
            )
            for n, (block, rows, device) in enumerate(plan)
        ]

    def stacked(ref, rows):
        return jnp.concatenate([ref[rows, :HD], ref[rows, HD:]], axis=0)

    def forward(i, carry):
        base = pl.multiple_of(i * TILE, TILE)
        rows = pl.ds(base, TILE)
        wide = pl.ds(base, WINDOW)
        low = low_ref[rows, :1] - base
        low = jnp.concatenate([low, low], axis=0)
        row = lax.broadcasted_iota(jnp.int32, (2 * TILE, 1), 0) % TILE
        col = lax.broadcasted_iota(jnp.int32, (2 * TILE, WINDOW), 1)
        scores = nt(stacked(q_ref, rows), keys[wide, :])
        before = jnp.where(col[:, :W] >= low, scores[:, :W], -1e30)
        edge = (col[:, W:] >= low) & (col[:, W:] <= row + W)
        scores = jnp.concatenate([before, jnp.where(edge, scores[:, W:], -1e30)], axis=1)
        top = jnp.max(scores, axis=-1, keepdims=True)
        raised = jnp.exp2((scores - top) * (scale * LOG2E))
        prob = raised * (1.0 / jnp.sum(raised, axis=-1, keepdims=True))
        probs[i] = prob
        result = nn(prob.astype(BF16), values[wide, :]).astype(BF16)
        attn[rows, :HD] = result[:TILE]
        attn[rows, HD:] = result[TILE:]
        return carry

    def backward(i, carry):
        base = pl.multiple_of(i * TILE, TILE)
        rows = pl.ds(base, TILE)
        wide = pl.ds(base, WINDOW)
        grad = stacked(dattn, rows)
        prob = probs[i]
        dprobs = nt(grad, values[wide, :])
        delta = jnp.sum(
            grad.astype(F32) * stacked(attn, rows).astype(F32), axis=-1, keepdims=True
        )
        dscores = (prob * (dprobs - delta) * scale).astype(BF16)
        dq = nn(dscores, keys[wide, :])
        lin[0, 0, rows, :HD] = rotate(dq[:TILE], cos_ref[rows, :], sin_ref[rows, :]).astype(BF16)
        lin[0, 0, rows, HD:] = rotate(
            dq[TILE:], cos_ref[rows, :], sin_ref[rows, :]
        ).astype(BF16)
        dkt[:, wide] += nn(stacked(q_ref, rows).T, dscores)
        dvt[:, wide] += nn(grad.T, prob.astype(BF16))
        return carry

    def outer_multiply():
        right = attn[...]

        def body(i, carry):
            lanes = pl.ds(pl.multiple_of(i * HALF, 128), HALF)
            result = lax.dot_general(
                og[:, lanes], right, (((0,), (0,)), ((), ())), preferred_element_type=F32
            ).astype(BF16)
            for j in range(8):
                rows = slice(OWN * j, OWN * j + OWN)
                parts[0, 8 * i + j] = result[rows, :HD]
                parts[1, 4 * (j % 4) + 2 * i + j // 4] = result[rows, HD:]
            return carry

        lax.fori_loop(0, 2, body, 0)

    def outer_first(kinds, order):
        for n in order:
            for kind in kinds:
                outer(kind)[n].start()

    def outer_second(kind):
        me = lines[kind][1]
        after = 4 * lax.rem(me + 1, 4)
        before = 4 * lax.rem(me + 3, 4)
        for n, start in ((0, after), (1, before + 2)):
            outer(kind)[n].wait_recv()
            where = pl.ds(start, 2)
            parts[kind, where] = (
                parts[kind, where].astype(F32) + near[kind, n].astype(F32)
            ).astype(BF16)
            outer(kind)[4 + n].start()

    def inner_start(s):
        for n in range(4):
            inner(s)[n].start()

    def outer_last(kind):
        me = lines[kind][1]
        for n in (2, 3, 4, 5):
            outer(kind)[n].wait_recv()
        for block in range(4):
            first, second = (4, 3) if block < 2 else (2, 5)
            mid_half[kind, block] = (
                parts[kind, 4 * me + block].astype(F32)
                + near[kind, first, block % 2].astype(F32)
                + near[kind, second, block % 2].astype(F32)
            ).astype(BF16)
        inner_start(kind)

    def inner_multiply(r, *blocks):
        for j in blocks:
            term = lax.dot_general(
                wide_x[j], lin[r, j], (((0,), (0,)), ((), ())), preferred_element_type=F32
            )
            product[...] = term if j == 0 else product[...] + term

    def inner_round(r):
        for block in range(4):
            start = pl.multiple_of(64 * lax.rem(z, 2) + OWN * block, 16)
            mid_full[r, block] = product[pl.ds(start, OWN), :].astype(BF16)
        inner_start(2 + r)

    def inner_second(s):
        _, me, mid, far = stages[s]
        after = lax.rem(me + 1, 4)
        before = lax.rem(me + 3, 4)
        for n, block, rows in ((0, after, upper), (1, before, lower)):
            inner(s)[n].wait_recv()
            mid[block, rows] = (
                mid[block, rows].astype(F32) + far[n, pl.ds(0, rows.size)].astype(F32)
            ).astype(BF16)
            inner(s)[4 + n].start()

    def inner_last(s, outs):
        _, me, mid, far = stages[s]
        for n in (2, 3, 4, 5):
            inner(s)[n].wait_recv()
        for rows, first, second in ((upper, 4, 3), (lower, 2, 5)):
            size = pl.ds(0, rows.size)
            total = (
                mid[me, rows].astype(F32) + far[first, size].astype(F32)
                + far[second, size].astype(F32)
            )
            for out, source, lanes in outs:
                out[rows, lanes] = total[:, source]

    there, after, before = lax.rem(chip + 2, 4), lax.rem(chip + 1, 4), lax.rem(chip + 3, 4)
    pair_copies = [
        remote(ig.at[1 - core, block], pair.at[block], f_send.at[n], f_recv.at[n], partner)
        for n, block in enumerate((there, after, before, chip))
    ]
    ring_x = [
        remote(ig.at[core, block, h], xring.at[n], g_send.at[n], g_recv.at[n], device)
        for n, (block, h, device) in enumerate((
            (there, 0, xplus), (there, 1, xminus), (after, 1, xplus), (before, 0, xminus),
            (after, 0, xplus), (before, 1, xminus),
        ))
    ]

    def query_multiply():
        for h in range(2):
            total = nt(lin[0, 0], wq[pl.ds(h * HALF, HALF), :]).astype(BF16)
            for o in range(8):
                ig[o % 2, o // 2, h] = total[64 * o : 64 * o + 64]

    def core_rows(which):
        return [
            lin[1, 0, pl.ds(pl.multiple_of(64 * (2 * n + which), 64), 64), :] for n in range(4)
        ]

    def key_multiply():
        left = jnp.concatenate(core_rows(core), axis=0)
        left = jnp.concatenate([left, swap_in[...]], axis=1)
        for n in range(4):
            pair_copies[n].wait_recv()
        for h in range(2):
            total = nt(left, wkv[pl.ds(h * HALF, HALF), :])
            for n in range(4):
                ig[core, n, h] = (
                    total[64 * n : 64 * n + 64] + ig[core, n, h].astype(F32)
                    + pair[n, h].astype(F32)
                ).astype(BF16)
            ring_x[h].start()

    def ring_second():
        for n, block in ((0, after), (1, before)):
            ring_x[n].wait_recv()
            ig[core, block, n] = (
                ig[core, block, n].astype(F32) + xring[n].astype(F32)
            ).astype(BF16)
            ring_x[4 + n].start()

    def ring_last():
        for n in (2, 3, 4, 5):
            ring_x[n].wait_recv()
        for h, first, second in ((0, 4, 3), (1, 2, 5)):
            ig_out[:, pl.ds(h * HALF, HALF)] = (
                ig[core, chip, h].astype(F32) + xring[first].astype(F32)
                + xring[second].astype(F32)
            ).astype(BF16)

    def store(n, src, dst):
        return pltpu.make_async_copy(src, dst, out_sem.at[n])

    store_ig = store(0, ig_out, ig_hbm)
    store_gq = store(1, gq_out, gq_hbm)
    store_gk = store(2, gk_out, gk_hbm)
    store_gv = store(3, gv_out, gv_hbm)
    store_go = store(4, go_out, go_hbm)

    for copy in ring_kv[:2] + (load_og, load_wo) + tuple(move_z):
        copy.start()
    for copy in (load_x, load_wk, load_wv) + tuple(move_w):
        copy.start()
    for copy in small[:2]:
        copy.wait()
    lane = lax.broadcasted_iota(jnp.int32, (TILE, HD), 1)
    for n in range(ROWS // TILE):
        rows = slice(TILE * n, TILE * n + TILE)
        place = jnp.broadcast_to(place_ref[n : n + 1, :].astype(F32), (TILE, HD)).T
        angle = place * freq_ref[...]
        cos_ref[rows, :] = jnp.cos(angle)
        sine = jnp.sin(angle)
        sin_ref[rows, :] = jnp.where(lane < HD // 2, sine, -sine)
        row = lax.broadcasted_iota(jnp.int32, (TILE, HD), 0) + TILE * n
        reach = jnp.minimum(place.astype(jnp.int32), W - 1)
        low_ref[rows, :] = jnp.maximum(row - reach + 2 * ROWS, (2 - y) * ROWS)
    dkt[...] = jnp.zeros_like(dkt)
    dvt[...] = jnp.zeros_like(dvt)
    ring_kv[0].wait_send()
    ring_kv[2].start()
    for n in range(2):
        ring_kv[n].wait_recv()
        ring_kv[3 + n].start()
    load_og.wait()
    load_wo.wait()
    dattn[...] = nn(og[...], wq[...]).astype(BF16)
    load_wq.start()
    for copy in move_z:
        copy.wait_recv()
    for copy in move_x[:2] + move_core[:1]:
        copy.start()
    for copy in small[2:]:
        copy.wait()
    for copy in ring_kv[2:]:
        copy.wait_recv()
    lax.fori_loop(0, ROWS // TILE, forward, 0)
    lax.fori_loop(0, ROWS // TILE, backward, 0)
    gout[0] = dkt[:, oldest].astype(BF16)
    gout[1] = dvt[:, oldest].astype(BF16)
    gout[2] = dvt[:, middle].astype(BF16)
    for copy in ring_back[:2] + tuple(gather(0)[:2]):
        copy.start()
    outer_multiply()
    outer_first((1,), (0,))
    ring_back[0].wait_send()
    ring_back[2].start()
    load_wq.wait()
    query_multiply()
    for copy in pair_copies:
        copy.start()
    outer_first((0,), (0, 1))
    ring_back[0].wait_recv()
    gin[0] = (gin[0].astype(F32) + dkt[:, middle]).astype(BF16)
    ring_back[3].start()
    ring_back[1].wait_recv()
    ring_back[4].start()
    load_x.wait()
    inner_multiply(0, 0)
    gather_relay(0)
    for n in range(2):
        move_x[n].wait_recv()
        move_x[2 + n].start()
        move_core[1 + n].start()
    for copy in ring_back[2:]:
        copy.wait_recv()
    key_grad = (dkt[:, latest] + gin[3].astype(F32)).T
    value_grad = (dvt[:, latest] + gin[2].astype(F32) + gin[4].astype(F32)).T
    lin[1, 0, :, :HD] = rotate(key_grad, cos_ref[...], sin_ref[...]).astype(BF16)
    lin[1, 0, :, HD:] = value_grad.astype(BF16)
    swap_out[...] = jnp.concatenate(core_rows(1 - core), axis=0)
    move_swap.start()
    for copy in gather(1)[:2]:
        copy.start()
    outer_first((1,), (1, 2, 3))
    load_wk.wait()
    load_wv.wait()
    for copy in move_w:
        copy.wait_recv()
    move_swap.wait_recv()
    key_multiply()
    for copy in move_x[2:]:
        copy.wait_recv()
    move_core[3].start()
    outer_first((0,), (2, 3))
    for copy in move_core + gather(0)[2:]:
        copy.wait_recv()
    inner_multiply(0, 3, 1, 2)
    inner_round(0)
    gather_relay(1)
    outer_second(1)
    inner_multiply(1, 0, 3, 1)
    for n in range(2):
        ring_x[n].wait_send()
        ring_x[2 + n].start()
    ring_second()
    outer_second(0)
    inner_second(2)
    for copy in gather(1)[2:]:
        copy.wait_recv()
    inner_multiply(1, 2)
    inner_round(1)
    outer_last(1)
    outer_last(0)
    inner_second(3)
    inner_second(1)
    inner_second(0)
    every = slice(0, 2 * HD)
    left, right = slice(0, HD), slice(HD, 2 * HD)
    inner_last(2, ((gq_out, every, every),))
    store_gq.start()
    inner_last(3, ((gk_out, left, left), (gv_out, right, left)))
    store_gk.start()
    store_gv.start()
    inner_last(1, ((go_out, left, right),))
    inner_last(0, ((go_out, left, left),))
    store_go.start()
    ring_last()
    store_ig.start()
    for copy in (store_go, store_gq, store_gk, store_gv, store_ig):
        copy.wait()
    sent = list(ring_kv[1:] + ring_back[1:]) + move_z + move_x + move_core + move_w + [move_swap]
    sent += pair_copies + ring_x[2:]
    for s in range(4):
        sent += inner(s)
    for n in range(2):
        sent += gather(n) + outer(n)
    for copy in sent:
        copy.wait_send()


OUTS = (
    jax.ShapeDtypeStruct((64, D), BF16),
    jax.ShapeDtypeStruct((OWN, 2 * HD), F32),
    jax.ShapeDtypeStruct((OWN, HD), F32),
    jax.ShapeDtypeStruct((OWN, HD), F32),
    jax.ShapeDtypeStruct((OWN, 2 * HD), F32),
)


def fused(*operands):
    anywhere = pl.BlockSpec(memory_space=pl.ANY)
    dma = pltpu.SemaphoreType.DMA
    buffers = (
        ((ROWS, HD), jnp.int32),
        ((ROWS, HD), F32),
        ((ROWS, HD), F32),
        ((ROWS, 2 * HD), BF16),
        ((ROWS // TILE, TILE), jnp.int32),
        ((1, HD), F32),
        ((BAND, HD), BF16),
        ((BAND, HD), BF16),
        ((ROWS, HD), BF16),
        ((ROWS, D), BF16),
        ((4, ROWS, SPAN), BF16),
        ((D, 2 * HD), BF16),
        ((D, 4 * HD), BF16),
        ((ROWS, 2 * HD), BF16),
        ((ROWS, 2 * HD), BF16),
        ((2, 4, ROWS, 2 * HD), BF16),
        ((ROWS // 2, 2 * HD), BF16),
        ((ROWS // 2, 2 * HD), BF16),
        ((ROWS // TILE, 2 * TILE, WINDOW), F32),
        ((HD, BAND), F32),
        ((HD, BAND), F32),
        ((3, HD, ROWS), BF16),
        ((5, HD, ROWS), BF16),
        ((SPAN, 2 * HD), F32),
        ((2, 16, OWN, HD), BF16),
        ((2, 6, 2, OWN, HD), BF16),
        ((2, 4, OWN, HD), BF16),
        ((2, 4, OWN, 2 * HD), BF16),
        ((2, 6, TOP, HD), BF16),
        ((2, 6, TOP, 2 * HD), BF16),
        ((2, 4, 2, 64, HALF), BF16),
        ((4, 2, 64, HALF), BF16),
        ((6, 64, HALF), BF16),
    )
    counts = ((5,), (5,), (2, 6), (4, 6), (4,), (6,), (14,), (2, 4))
    return pl.pallas_call(
        fused_kernel,
        out_shape=OUTS,
        in_specs=[anywhere] * 11,
        out_specs=(anywhere,) * 5,
        scratch_shapes=[pltpu.VMEM(out.shape, out.dtype) for out in OUTS]
        + [pltpu.VMEM(*buffer) for buffer in buffers]
        + [dma((13,)), dma((5,))]
        + [dma(count) for count in counts for _ in range(2)],
        compiler_params=pltpu.CompilerParams(
            collective_id=0, has_side_effects=True, vmem_limit_bytes=66_900_000
        ),
        name="fused",
    )(*operands)


def finish_kernel(*refs):
    sources, targets, buffers, sems = refs[:5], refs[5:10], refs[10:15], refs[15]
    order = (0, 1, 4, 2, 3)
    loads = [pltpu.make_async_copy(sources[n], buffers[n], sems.at[0, n]) for n in range(5)]
    stores = [pltpu.make_async_copy(buffers[n], targets[n], sems.at[1, n]) for n in range(5)]
    for n in order:
        loads[n].start()
    for n in order:
        loads[n].wait()
        stores[n].start()
    for n in order:
        stores[n].wait()


def finish(*results):
    anywhere = pl.BlockSpec(memory_space=pl.ANY)
    return pl.pallas_call(
        finish_kernel, out_shape=OUTS, in_specs=[anywhere] * 5, out_specs=(anywhere,) * 5,
        scratch_shapes=[pltpu.VMEM(out.shape, out.dtype) for out in OUTS]
        + [pltpu.SemaphoreType.DMA((2, 5))],
        compiler_params=pltpu.CompilerParams(vmem_limit_bytes=66_900_000),
        name="finish",
    )(*results)


def on_device(
    inputs, queries, key_states, value_states, out_grad, positions,
    w_query, w_key, w_value, w_output,
):
    index = np.arange(HD) % (HD // 2)
    freq = jnp.asarray((10000.0 ** (index * (-2.0 / HD))).astype(np.float32)[None, :])
    return finish(
        *fused(
            queries, key_states, value_states, positions.reshape(ROWS // TILE, TILE), freq,
            inputs, out_grad, w_query, w_key, w_value, w_output,
        )
    )


def solution(mesh):
    rows = ("dp", "context")
    return jax.shard_map(
        on_device,
        mesh=mesh,
        in_specs=(
            P(rows, None), P(rows, "tensor"), P(rows, "tensor"), P(rows, "tensor"),
            P(rows, None), P(rows), P(None, "tensor"), P(None, "tensor"),
            P(None, "tensor"), P(None, "tensor"),
        ),
        out_specs=(
            P(("dp", "context", "tensor"), None), P(rows, "tensor"), P(rows, "tensor"),
            P(rows, "tensor"), P(rows, "tensor"),
        ),
        check_vma=False,
    )
```

```python
import functools

import jax
import jax.numpy as jnp
import numpy as np
from jax import lax
from jax.experimental import pallas as pl
from jax.experimental.pallas import tpu as pltpu
from jax.sharding import PartitionSpec as P

HD = 128
W = 1024
QSCALAR = 168
D = 5376
ROWS = 512
TILE = 128
WINDOW = W + TILE
BAND = 3 * ROWS
OWN = D // 16
HALF = D // 2
SPAN = 1408
TOP = 176
LOG2E = 1.4426950408889634
F32 = jnp.float32
BF16 = jnp.bfloat16
MESH = pl.DeviceIdType.MESH


def nt(left, right):
    return lax.dot_general(left, right, (((1,), (1,)), ((), ())), preferred_element_type=F32)


def nn(left, right):
    return jnp.dot(left, right, preferred_element_type=F32)


def rotate(grad, cosine, sine):
    return grad * cosine + pltpu.roll(grad, HD // 2, 1) * sine


def step(axis, index, delta):
    size = 4
    return {axis: lax.rem(index + delta + size, size)}


def fused_kernel(
    q_hbm, k_hbm, v_hbm, place_hbm, freq_hbm,
    x_hbm, og_hbm, wq_hbm, wk_hbm, wv_hbm, wo_hbm,
    ig_hbm, gq_hbm, gk_hbm, gv_hbm, go_hbm,
    ig_out, gq_out, gk_out, gv_out, go_out, low_ref, cos_ref, sin_ref,
    q_ref, place_ref, freq_ref, keys, values, relay, og, wide_x, wq, wkv, dattn, attn, lin, swap_out, swap_in,
    probs, dkt, dvt, gout, gin, product,
    parts, near, mid_half, mid_full, far_half, far_full, ig, pair, xring, load_sem, out_sem,
    a_send, a_recv, b_send, b_recv, c_send, c_recv, e_send, e_recv,
    f_send, f_recv, g_send, g_recv, h_send, h_recv, l_send, l_recv,
):
    scale = QSCALAR ** (-0.5)
    z = lax.axis_index("dp")
    y = lax.axis_index("context")
    t = lax.axis_index("tensor")
    core = lax.rem(t, 2)
    chip = t // 2
    partner = {"tensor": t + 1 - 2 * core}
    tplus, tminus, tfar = lax.rem(t + 2, 8), lax.rem(t + 6, 8), lax.rem(t + 4, 8)
    xplus, xminus = {"tensor": tplus}, {"tensor": tminus}
    yplus, yminus = step("context", y, 1), step("context", y, -1)
    zplus, zminus, zfar = step("dp", z, 1), step("dp", z, -1), step("dp", z, 2)
    oldest, middle, latest = pl.ds(0, ROWS), pl.ds(ROWS, ROWS), pl.ds(2 * ROWS, ROWS)

    def load(n, src, dst):
        return pltpu.make_async_copy(src, dst, load_sem.at[n])

    def columns(delta):
        there = lax.rem(z + delta, 4)
        return pl.ds(pl.multiple_of(4 * OWN * there - 64 * lax.rem(there, 2), 128), SPAN)

    load_og = load(0, og_hbm, og)
    load_wo = load(1, wo_hbm, wq)
    load_x = load(4, x_hbm.at[:, columns(0)], wide_x.at[0])
    load_wq = load(5, wq_hbm, wq)
    load_wk = load(6, wk_hbm, wkv.at[:, pl.ds(0, HD)])
    load_wv = load(7, wv_hbm, wkv.at[:, pl.ds(HD, HD)])
    small = [
        load(8 + n, src, dst)
        for n, (src, dst) in enumerate((
            (place_hbm, place_ref), (freq_hbm, freq_ref), (q_hbm, q_ref),
            (k_hbm, keys.at[latest]), (v_hbm, values.at[latest]),
        ))
    ]
    barrier = pltpu.get_barrier_semaphore()
    for device in (zfar, yplus, yminus, zplus, zminus, xplus, xminus, partner):
        pl.semaphore_signal(barrier, inc=1, device_id=device, device_id_type=MESH)
    for copy in small:
        copy.start()
    pl.semaphore_wait(barrier, 8)

    lines = (("dp", z, "context", y), ("context", y, "dp", z))

    def remote(src, dst, send, recv, device):
        return pltpu.make_async_remote_copy(
            src_ref=src, dst_ref=dst, send_sem=send, recv_sem=recv,
            device_id=device, device_id_type=MESH,
        )

    def ring(n, src, dst, device):
        return remote(src, dst, a_send.at[n], a_recv.at[n], device)

    ring_kv = (
        ring(0, k_hbm, keys.at[middle], yplus),
        ring(1, v_hbm, relay, yminus),
        ring(2, v_hbm, values.at[middle], yplus),
        ring(3, keys.at[middle], keys.at[oldest], yplus),
        ring(4, relay, values.at[oldest], yminus),
    )

    def back(n, src, dst, device):
        return remote(gout.at[src] if src < 3 else gin.at[src - 3], gin.at[dst],
                      b_send.at[n], b_recv.at[n], device)

    ring_back = (
        back(0, 0, 0, yminus), back(1, 1, 1, yplus), back(2, 2, 2, yminus),
        back(3, 3, 3, yminus), back(4, 4, 4, yplus),
    )

    def eighth(where, start=0, size=64):
        return wide_x.at[pl.ds(1, 3), pl.ds(pl.multiple_of(64 * where + start, 16), size)]

    def move(n, src, dst, device):
        return remote(src, dst, h_send.at[n], h_recv.at[n], device)

    mine = pl.ds(pl.multiple_of(64 * t, 64), 64)
    move_z = [
        move(n, x_hbm.at[mine, columns(delta)], wide_x.at[4 - delta, mine], device)
        for n, (delta, device) in enumerate(((1, zplus), (3, zminus), (2, zfar)))
    ]
    move_x = [
        move(3, eighth(t), eighth(t), xplus),
        move(4, eighth(t), eighth(t), xminus),
        move(5, eighth(tminus, 0, 32), eighth(tminus, 0, 32), xplus),
        move(6, eighth(tplus, 32, 32), eighth(tplus, 32, 32), xminus),
    ]
    move_core = [
        move(7 + n, eighth(where), eighth(where), partner)
        for n, where in enumerate((t, tminus, tplus, tfar))
    ]
    move_w = [
        move(11, wk_hbm, wkv.at[:, pl.ds(2 * HD, HD)], partner),
        move(12, wv_hbm, wkv.at[:, pl.ds(3 * HD, HD)], partner),
    ]
    move_swap = move(13, swap_out, swap_in, partner)

    @functools.cache
    def gather(r):
        first, second = pl.ds(0, ROWS // 2), pl.ds(ROWS // 2, ROWS // 2)
        plan = (
            (lin.at[r, 0], lin.at[r, 3], zplus),
            (lin.at[r, 0], lin.at[r, 1], zminus),
            (lin.at[r, 3, first], lin.at[r, 2, first], zplus),
            (lin.at[r, 1, second], lin.at[r, 2, second], zminus),
        )
        return [
            remote(src, dst, l_send.at[r, n], l_recv.at[r, n], device)
            for n, (src, dst, device) in enumerate(plan)
        ]

    def gather_relay(r):
        for n in range(2):
            gather(r)[n].wait_recv()
            gather(r)[2 + n].start()

    @functools.cache
    def outer(kind):
        axis, me, _, _ = lines[kind]
        there = 4 * lax.rem(me + 2, 4)
        after = 4 * lax.rem(me + 1, 4)
        before = 4 * lax.rem(me + 3, 4)
        up, down = step(axis, me, 1), step(axis, me, -1)
        plan = (
            (there, up), (there + 2, down), (after + 2, up), (before, down),
            (after, up), (before + 2, down),
        )
        return [
            remote(
                parts.at[kind, pl.ds(start, 2)], near.at[kind, n],
                c_send.at[kind, n], c_recv.at[kind, n], device,
            )
            for n, (start, device) in enumerate(plan)
        ]

    upper, lower = pl.ds(0, TOP), pl.ds(TOP, OWN - TOP)
    stages = (
        ("context", y, mid_half.at[0], far_half.at[0]),
        ("dp", z, mid_half.at[1], far_half.at[1]),
        ("context", y, mid_full.at[0], far_full.at[0]),
        ("context", y, mid_full.at[1], far_full.at[1]),
    )

    @functools.cache
    def inner(s):
        axis, me, mid, far = stages[s]
        there = lax.rem(me + 2, 4)
        after = lax.rem(me + 1, 4)
        before = lax.rem(me + 3, 4)
        up, down = step(axis, me, 1), step(axis, me, -1)
        plan = (
            (there, upper, up), (there, lower, down), (after, lower, up), (before, upper, down),
            (after, upper, up), (before, lower, down),
        )
        return [
            remote(
                mid.at[block, rows], far.at[n, pl.ds(0, rows.size)],
                e_send.at[s, n], e_recv.at[s, n], device,
            )
            for n, (block, rows, device) in enumerate(plan)
        ]

    def stacked(ref, rows):
        return jnp.concatenate([ref[rows, :HD], ref[rows, HD:]], axis=0)

    def forward(i, carry):
        base = pl.multiple_of(i * TILE, TILE)
        rows = pl.ds(base, TILE)
        wide = pl.ds(base, WINDOW)
        low = low_ref[rows, :1] - base
        low = jnp.concatenate([low, low], axis=0)
        row = lax.broadcasted_iota(jnp.int32, (2 * TILE, 1), 0) % TILE
        col = lax.broadcasted_iota(jnp.int32, (2 * TILE, WINDOW), 1)
        scores = nt(stacked(q_ref, rows), keys[wide, :])
        before = jnp.where(col[:, :W] >= low, scores[:, :W], -1e30)
        edge = (col[:, W:] >= low) & (col[:, W:] <= row + W)
        scores = jnp.concatenate([before, jnp.where(edge, scores[:, W:], -1e30)], axis=1)
        top = jnp.max(scores, axis=-1, keepdims=True)
        raised = jnp.exp2((scores - top) * (scale * LOG2E))
        prob = raised * (1.0 / jnp.sum(raised, axis=-1, keepdims=True))
        probs[i] = prob
        half = prob.astype(BF16)
        result = nn(half, values[wide, :]).astype(BF16)
        dvt[:, wide] += nn(stacked(dattn, rows).T, half)
        attn[rows, :HD] = result[:TILE]
        attn[rows, HD:] = result[TILE:]
        return carry

    def backward(i, carry):
        base = pl.multiple_of(i * TILE, TILE)
        rows = pl.ds(base, TILE)
        wide = pl.ds(base, WINDOW)
        grad = stacked(dattn, rows)
        prob = probs[i]
        dprobs = nt(grad, values[wide, :])
        delta = jnp.sum(
            grad.astype(F32) * stacked(attn, rows).astype(F32), axis=-1, keepdims=True
        )
        dscores = (prob * (dprobs - delta) * scale).astype(BF16)
        dq = nn(dscores, keys[wide, :])
        lin[0, 0, rows, :HD] = rotate(dq[:TILE], cos_ref[rows, :], sin_ref[rows, :]).astype(BF16)
        lin[0, 0, rows, HD:] = rotate(
            dq[TILE:], cos_ref[rows, :], sin_ref[rows, :]
        ).astype(BF16)
        dkt[:, wide] += nn(stacked(q_ref, rows).T, dscores)
        return carry

    def outer_multiply():
        right = attn[...]

        def body(i, carry):
            lanes = pl.ds(pl.multiple_of(i * HALF, 128), HALF)
            result = lax.dot_general(
                og[:, lanes], right, (((0,), (0,)), ((), ())), preferred_element_type=F32
            ).astype(BF16)
            for j in range(8):
                rows = slice(OWN * j, OWN * j + OWN)
                parts[0, 8 * i + j] = result[rows, :HD]
                parts[1, 4 * (j % 4) + 2 * i + j // 4] = result[rows, HD:]
            return carry

        lax.fori_loop(0, 2, body, 0)

    def outer_first(kinds, order):
        for n in order:
            for kind in kinds:
                outer(kind)[n].start()

    def outer_second(kind):
        me = lines[kind][1]
        after = 4 * lax.rem(me + 1, 4)
        before = 4 * lax.rem(me + 3, 4)
        for n, start in ((0, after), (1, before + 2)):
            outer(kind)[n].wait_recv()
            where = pl.ds(start, 2)
            parts[kind, where] = (
                parts[kind, where].astype(F32) + near[kind, n].astype(F32)
            ).astype(BF16)
            outer(kind)[4 + n].start()

    def inner_start(s):
        for n in range(4):
            inner(s)[n].start()

    def outer_last(kind):
        me = lines[kind][1]
        for n in (2, 3, 4, 5):
            outer(kind)[n].wait_recv()
        for block in range(4):
            first, second = (4, 3) if block < 2 else (2, 5)
            mid_half[kind, block] = (
                parts[kind, 4 * me + block].astype(F32)
                + near[kind, first, block % 2].astype(F32)
                + near[kind, second, block % 2].astype(F32)
            ).astype(BF16)
        inner_start(kind)

    def inner_multiply(r, *blocks):
        for j in blocks:
            term = lax.dot_general(
                wide_x[j], lin[r, j], (((0,), (0,)), ((), ())), preferred_element_type=F32
            )
            product[...] = term if j == 0 else product[...] + term

    def inner_round(r):
        for block in range(4):
            start = pl.multiple_of(64 * lax.rem(z, 2) + OWN * block, 16)
            mid_full[r, block] = product[pl.ds(start, OWN), :].astype(BF16)
        inner_start(2 + r)

    def inner_second(s):
        _, me, mid, far = stages[s]
        after = lax.rem(me + 1, 4)
        before = lax.rem(me + 3, 4)
        for n, block, rows in ((0, after, upper), (1, before, lower)):
            inner(s)[n].wait_recv()
            mid[block, rows] = (
                mid[block, rows].astype(F32) + far[n, pl.ds(0, rows.size)].astype(F32)
            ).astype(BF16)
            inner(s)[4 + n].start()

    def inner_last(s, outs):
        _, me, mid, far = stages[s]
        for n in (2, 3, 4, 5):
            inner(s)[n].wait_recv()
        for rows, first, second in ((upper, 4, 3), (lower, 2, 5)):
            size = pl.ds(0, rows.size)
            total = (
                mid[me, rows].astype(F32) + far[first, size].astype(F32)
                + far[second, size].astype(F32)
            )
            for out, source, lanes in outs:
                out[rows, lanes] = total[:, source]

    there, after, before = lax.rem(chip + 2, 4), lax.rem(chip + 1, 4), lax.rem(chip + 3, 4)
    pair_copies = [
        remote(ig.at[1 - core, block], pair.at[block], f_send.at[n], f_recv.at[n], partner)
        for n, block in enumerate((there, after, before, chip))
    ]
    ring_x = [
        remote(ig.at[core, block, h], xring.at[n], g_send.at[n], g_recv.at[n], device)
        for n, (block, h, device) in enumerate((
            (there, 0, xplus), (there, 1, xminus), (after, 1, xplus), (before, 0, xminus),
            (after, 0, xplus), (before, 1, xminus),
        ))
    ]

    def query_multiply():
        for h in range(2):
            total = nt(lin[0, 0], wq[pl.ds(h * HALF, HALF), :]).astype(BF16)
            for o in range(8):
                ig[o % 2, o // 2, h] = total[64 * o : 64 * o + 64]

    def core_rows(which):
        return [
            lin[1, 0, pl.ds(pl.multiple_of(64 * (2 * n + which), 64), 64), :] for n in range(4)
        ]

    def key_multiply():
        left = jnp.concatenate(core_rows(core), axis=0)
        left = jnp.concatenate([left, swap_in[...]], axis=1)
        for n in range(4):
            pair_copies[n].wait_recv()
        for h in range(2):
            total = nt(left, wkv[pl.ds(h * HALF, HALF), :])
            for n in range(4):
                ig[core, n, h] = (
                    total[64 * n : 64 * n + 64] + ig[core, n, h].astype(F32)
                    + pair[n, h].astype(F32)
                ).astype(BF16)
            ring_x[h].start()

    def ring_second():
        for n, block in ((0, after), (1, before)):
            ring_x[n].wait_recv()
            ig[core, block, n] = (
                ig[core, block, n].astype(F32) + xring[n].astype(F32)
            ).astype(BF16)
            ring_x[4 + n].start()

    def ring_last():
        for n in (2, 3, 4, 5):
            ring_x[n].wait_recv()
        for h, first, second in ((0, 4, 3), (1, 2, 5)):
            ig_out[:, pl.ds(h * HALF, HALF)] = (
                ig[core, chip, h].astype(F32) + xring[first].astype(F32)
                + xring[second].astype(F32)
            ).astype(BF16)

    def store(n, src, dst):
        return pltpu.make_async_copy(src, dst, out_sem.at[n])

    store_ig = store(0, ig_out, ig_hbm)
    store_gq = store(1, gq_out, gq_hbm)
    store_gk = store(2, gk_out, gk_hbm)
    store_gv = store(3, gv_out, gv_hbm)
    store_go = store(4, go_out, go_hbm)

    for copy in ring_kv[:2] + (load_og, load_wo) + tuple(move_z):
        copy.start()
    for copy in (load_x, load_wk, load_wv) + tuple(move_w):
        copy.start()
    for copy in small[:2]:
        copy.wait()
    lane = lax.broadcasted_iota(jnp.int32, (TILE, HD), 1)
    for n in range(ROWS // TILE):
        rows = slice(TILE * n, TILE * n + TILE)
        place = jnp.broadcast_to(place_ref[n : n + 1, :].astype(F32), (TILE, HD)).T
        angle = place * freq_ref[...]
        cos_ref[rows, :] = jnp.cos(angle)
        sine = jnp.sin(angle)
        sin_ref[rows, :] = jnp.where(lane < HD // 2, sine, -sine)
        row = lax.broadcasted_iota(jnp.int32, (TILE, HD), 0) + TILE * n
        reach = jnp.minimum(place.astype(jnp.int32), W - 1)
        low_ref[rows, :] = jnp.maximum(row - reach + 2 * ROWS, (2 - y) * ROWS)
    dkt[...] = jnp.zeros_like(dkt)
    dvt[...] = jnp.zeros_like(dvt)
    ring_kv[0].wait_send()
    ring_kv[2].start()
    for n in range(2):
        ring_kv[n].wait_recv()
        ring_kv[3 + n].start()
    load_og.wait()
    load_wo.wait()
    dattn[...] = nn(og[...], wq[...]).astype(BF16)
    load_wq.start()
    for copy in small[2:]:
        copy.wait()
    for copy in ring_kv[2:]:
        copy.wait_recv()
    lax.fori_loop(0, 2, forward, 0, unroll=True)
    for copy in move_z:
        copy.wait_recv()
    for copy in move_x[:2] + move_core[:1]:
        copy.start()
    lax.fori_loop(2, ROWS // TILE, forward, 0, unroll=True)
    gout[1] = dvt[:, oldest].astype(BF16)
    gout[2] = dvt[:, middle].astype(BF16)
    for copy in ring_back[1:3]:
        copy.start()
    lax.fori_loop(0, ROWS // TILE, backward, 0, unroll=True)
    gout[0] = dkt[:, oldest].astype(BF16)
    for copy in ring_back[:1] + tuple(gather(0)[:2]):
        copy.start()
    outer_multiply()
    ring_back[1].wait_recv()
    ring_back[4].start()
    load_wq.wait()
    query_multiply()
    for copy in pair_copies:
        copy.start()
    outer_first((0,), (0, 1))
    ring_back[0].wait_recv()
    gin[0] = (gin[0].astype(F32) + dkt[:, middle]).astype(BF16)
    ring_back[3].start()
    load_x.wait()
    inner_multiply(0, 0)
    for n in range(2):
        move_x[n].wait_recv()
        move_x[2 + n].start()
    outer_first((1,), (0,))
    gather_relay(0)
    for copy in ring_back[2:]:
        copy.wait_recv()
    key_grad = (dkt[:, latest] + gin[3].astype(F32)).T
    value_grad = (dvt[:, latest] + gin[2].astype(F32) + gin[4].astype(F32)).T
    lin[1, 0, :, :HD] = rotate(key_grad, cos_ref[...], sin_ref[...]).astype(BF16)
    lin[1, 0, :, HD:] = value_grad.astype(BF16)
    swap_out[...] = jnp.concatenate(core_rows(1 - core), axis=0)
    move_swap.start()
    for copy in move_core[1:3]:
        copy.start()
    for copy in gather(1)[:2]:
        copy.start()
    load_wk.wait()
    load_wv.wait()
    for copy in move_w:
        copy.wait_recv()
    move_swap.wait_recv()
    outer_first((1,), (1, 2, 3))
    key_multiply()
    for copy in move_x[2:]:
        copy.wait_recv()
    move_core[3].start()
    outer_first((0,), (2, 3))
    for copy in move_core + gather(0)[2:]:
        copy.wait_recv()
    inner_multiply(0, 3, 1, 2)
    inner_round(0)
    for n in range(2):
        ring_x[n].wait_send()
        ring_x[2 + n].start()
    gather_relay(1)
    ring_second()
    outer_second(1)
    inner_multiply(1, 0, 3, 1)
    outer_second(0)
    inner_second(2)
    for copy in gather(1)[2:]:
        copy.wait_recv()
    inner_multiply(1, 2)
    inner_round(1)
    outer_last(1)
    outer_last(0)
    inner_second(3)
    inner_second(1)
    inner_second(0)
    every = slice(0, 2 * HD)
    left, right = slice(0, HD), slice(HD, 2 * HD)
    inner_last(2, ((gq_out, every, every),))
    store_gq.start()
    inner_last(3, ((gk_out, left, left), (gv_out, right, left)))
    store_gk.start()
    store_gv.start()
    inner_last(1, ((go_out, left, right),))
    inner_last(0, ((go_out, left, left),))
    store_go.start()
    ring_last()
    store_ig.start()
    for copy in (store_go, store_gq, store_gk, store_gv, store_ig):
        copy.wait()
    sent = list(ring_kv[1:] + ring_back) + move_z + move_x + move_core + move_w + [move_swap]
    sent += pair_copies + ring_x[2:]
    for s in range(4):
        sent += inner(s)
    for n in range(2):
        sent += gather(n) + outer(n)
    for copy in sent:
        copy.wait_send()


OUTS = (
    jax.ShapeDtypeStruct((64, D), BF16),
    jax.ShapeDtypeStruct((OWN, 2 * HD), F32),
    jax.ShapeDtypeStruct((OWN, HD), F32),
    jax.ShapeDtypeStruct((OWN, HD), F32),
    jax.ShapeDtypeStruct((OWN, 2 * HD), F32),
)


def fused(*operands):
    anywhere = pl.BlockSpec(memory_space=pl.ANY)
    dma = pltpu.SemaphoreType.DMA
    buffers = (
        ((ROWS, HD), jnp.int32),
        ((ROWS, HD), F32),
        ((ROWS, HD), F32),
        ((ROWS, 2 * HD), BF16),
        ((ROWS // TILE, TILE), jnp.int32),
        ((1, HD), F32),
        ((BAND, HD), BF16),
        ((BAND, HD), BF16),
        ((ROWS, HD), BF16),
        ((ROWS, D), BF16),
        ((4, ROWS, SPAN), BF16),
        ((D, 2 * HD), BF16),
        ((D, 4 * HD), BF16),
        ((ROWS, 2 * HD), BF16),
        ((ROWS, 2 * HD), BF16),
        ((2, 4, ROWS, 2 * HD), BF16),
        ((ROWS // 2, 2 * HD), BF16),
        ((ROWS // 2, 2 * HD), BF16),
        ((ROWS // TILE, 2 * TILE, WINDOW), F32),
        ((HD, BAND), F32),
        ((HD, BAND), F32),
        ((3, HD, ROWS), BF16),
        ((5, HD, ROWS), BF16),
        ((SPAN, 2 * HD), F32),
        ((2, 16, OWN, HD), BF16),
        ((2, 6, 2, OWN, HD), BF16),
        ((2, 4, OWN, HD), BF16),
        ((2, 4, OWN, 2 * HD), BF16),
        ((2, 6, TOP, HD), BF16),
        ((2, 6, TOP, 2 * HD), BF16),
        ((2, 4, 2, 64, HALF), BF16),
        ((4, 2, 64, HALF), BF16),
        ((6, 64, HALF), BF16),
    )
    counts = ((5,), (5,), (2, 6), (4, 6), (4,), (6,), (14,), (2, 4))
    return pl.pallas_call(
        fused_kernel,
        out_shape=OUTS,
        in_specs=[anywhere] * 11,
        out_specs=(anywhere,) * 5,
        scratch_shapes=[pltpu.VMEM(out.shape, out.dtype) for out in OUTS]
        + [pltpu.VMEM(*buffer) for buffer in buffers]
        + [dma((13,)), dma((5,))]
        + [dma(count) for count in counts for _ in range(2)],
        compiler_params=pltpu.CompilerParams(
            collective_id=0, has_side_effects=True, vmem_limit_bytes=66_900_000
        ),
        name="fused",
    )(*operands)


def finish_kernel(*refs):
    sources, targets, buffers, sems = refs[:5], refs[5:10], refs[10:15], refs[15]
    order = (0, 1, 4, 2, 3)
    loads = [pltpu.make_async_copy(sources[n], buffers[n], sems.at[0, n]) for n in range(5)]
    stores = [pltpu.make_async_copy(buffers[n], targets[n], sems.at[1, n]) for n in range(5)]
    for n in order:
        loads[n].start()
    for n in order:
        loads[n].wait()
        stores[n].start()
    for n in order:
        stores[n].wait()


def finish(*results):
    anywhere = pl.BlockSpec(memory_space=pl.ANY)
    return pl.pallas_call(
        finish_kernel, out_shape=OUTS, in_specs=[anywhere] * 5, out_specs=(anywhere,) * 5,
        scratch_shapes=[pltpu.VMEM(out.shape, out.dtype) for out in OUTS]
        + [pltpu.SemaphoreType.DMA((2, 5))],
        compiler_params=pltpu.CompilerParams(vmem_limit_bytes=66_900_000),
        name="finish",
    )(*results)


def on_device(
    inputs, queries, key_states, value_states, out_grad, positions,
    w_query, w_key, w_value, w_output,
):
    index = np.arange(HD) % (HD // 2)
    freq = jnp.asarray((10000.0 ** (index * (-2.0 / HD))).astype(np.float32)[None, :])
    return finish(
        *fused(
            queries, key_states, value_states, positions.reshape(ROWS // TILE, TILE), freq,
            inputs, out_grad, w_query, w_key, w_value, w_output,
        )
    )


def solution(mesh):
    rows = ("dp", "context")
    return jax.shard_map(
        on_device,
        mesh=mesh,
        in_specs=(
            P(rows, None), P(rows, "tensor"), P(rows, "tensor"), P(rows, "tensor"),
            P(rows, None), P(rows), P(None, "tensor"), P(None, "tensor"),
            P(None, "tensor"), P(None, "tensor"),
        ),
        out_specs=(
            P(("dp", "context", "tensor"), None), P(rows, "tensor"), P(rows, "tensor"),
            P(rows, "tensor"), P(rows, "tensor"),
        ),
        check_vma=False,
    )
```

```python
import functools

import jax
import jax.numpy as jnp
import numpy as np
from jax import lax
from jax.experimental import pallas as pl
from jax.experimental.pallas import tpu as pltpu
from jax.sharding import PartitionSpec as P

HD = 128
W = 1024
QSCALAR = 168
D = 5376
ROWS = 512
TILE = 128
WINDOW = W + TILE
BAND = 3 * ROWS
OWN = D // 16
HALF = D // 2
SPAN = 1408
TOP = 176
LOG2E = 1.4426950408889634
F32 = jnp.float32
BF16 = jnp.bfloat16
MESH = pl.DeviceIdType.MESH


def nt(left, right):
    return lax.dot_general(left, right, (((1,), (1,)), ((), ())), preferred_element_type=F32)


def nn(left, right):
    return jnp.dot(left, right, preferred_element_type=F32)


def rotate(grad, cosine, sine):
    return grad * cosine + pltpu.roll(grad, HD // 2, 1) * sine


def step(axis, index, delta):
    size = 4
    return {axis: lax.rem(index + delta + size, size)}


def fused_kernel(
    q_hbm, k_hbm, v_hbm, place_hbm, freq_hbm,
    x_hbm, og_hbm, wq_hbm, wk_hbm, wv_hbm, wo_hbm,
    ig_out, gq_out, gk_out, gv_out, go_out, low_ref, cos_ref, sin_ref,
    q_ref, place_ref, freq_ref, keys, values, relay, og, wide_x, wq, wkv, dattn, attn, lin, swap_out, swap_in,
    probs, dkt, dvt, gout, gin, product,
    parts, near, mid_half, mid_full, far_half, far_full, ig, pair, xring, load_sem,
    a_send, a_recv, b_send, b_recv, c_send, c_recv, e_send, e_recv,
    f_send, f_recv, g_send, g_recv, h_send, h_recv, l_send, l_recv,
):
    scale = QSCALAR ** (-0.5)
    z = lax.axis_index("dp")
    y = lax.axis_index("context")
    t = lax.axis_index("tensor")
    core = lax.rem(t, 2)
    chip = t // 2
    partner = {"tensor": t + 1 - 2 * core}
    tplus, tminus, tfar = lax.rem(t + 2, 8), lax.rem(t + 6, 8), lax.rem(t + 4, 8)
    xplus, xminus = {"tensor": tplus}, {"tensor": tminus}
    yplus, yminus = step("context", y, 1), step("context", y, -1)
    zplus, zminus, zfar = step("dp", z, 1), step("dp", z, -1), step("dp", z, 2)
    oldest, middle, latest = pl.ds(0, ROWS), pl.ds(ROWS, ROWS), pl.ds(2 * ROWS, ROWS)

    def load(n, src, dst):
        return pltpu.make_async_copy(src, dst, load_sem.at[n])

    def columns(delta):
        there = lax.rem(z + delta, 4)
        return pl.ds(pl.multiple_of(4 * OWN * there - 64 * lax.rem(there, 2), 128), SPAN)

    load_og = load(0, og_hbm, og)
    load_wo = load(1, wo_hbm, wq)
    load_x = load(4, x_hbm.at[:, columns(0)], wide_x.at[0])
    load_wq = load(5, wq_hbm, wq)
    load_wk = load(6, wk_hbm, wkv.at[:, pl.ds(0, HD)])
    load_wv = load(7, wv_hbm, wkv.at[:, pl.ds(HD, HD)])
    small = [
        load(8 + n, src, dst)
        for n, (src, dst) in enumerate((
            (place_hbm, place_ref), (freq_hbm, freq_ref), (q_hbm, q_ref),
            (k_hbm, keys.at[latest]), (v_hbm, values.at[latest]),
        ))
    ]
    barrier = pltpu.get_barrier_semaphore()
    for device in (zfar, yplus, yminus, zplus, zminus, xplus, xminus, partner):
        pl.semaphore_signal(barrier, inc=1, device_id=device, device_id_type=MESH)
    for copy in small:
        copy.start()
    pl.semaphore_wait(barrier, 8)

    lines = (("dp", z, "context", y), ("context", y, "dp", z))

    def remote(src, dst, send, recv, device):
        return pltpu.make_async_remote_copy(
            src_ref=src, dst_ref=dst, send_sem=send, recv_sem=recv,
            device_id=device, device_id_type=MESH,
        )

    def ring(n, src, dst, device):
        return remote(src, dst, a_send.at[n], a_recv.at[n], device)

    ring_kv = (
        ring(0, k_hbm, keys.at[middle], yplus),
        ring(1, v_hbm, relay, yminus),
        ring(2, v_hbm, values.at[middle], yplus),
        ring(3, keys.at[middle], keys.at[oldest], yplus),
        ring(4, relay, values.at[oldest], yminus),
    )

    def back(n, src, dst, device):
        return remote(gout.at[src] if src < 3 else gin.at[src - 3], gin.at[dst],
                      b_send.at[n], b_recv.at[n], device)

    ring_back = (
        back(0, 0, 0, yminus), back(1, 1, 1, yplus), back(2, 2, 2, yminus),
        back(3, 3, 3, yminus), back(4, 4, 4, yplus),
    )

    def eighth(where, start=0, size=64):
        return wide_x.at[pl.ds(1, 3), pl.ds(pl.multiple_of(64 * where + start, 16), size)]

    def move(n, src, dst, device):
        return remote(src, dst, h_send.at[n], h_recv.at[n], device)

    mine = pl.ds(pl.multiple_of(64 * t, 64), 64)
    move_z = [
        move(n, x_hbm.at[mine, columns(delta)], wide_x.at[4 - delta, mine], device)
        for n, (delta, device) in enumerate(((1, zplus), (3, zminus), (2, zfar)))
    ]
    move_x = [
        move(3, eighth(t), eighth(t), xplus),
        move(4, eighth(t), eighth(t), xminus),
        move(5, eighth(tminus, 0, 32), eighth(tminus, 0, 32), xplus),
        move(6, eighth(tplus, 32, 32), eighth(tplus, 32, 32), xminus),
    ]
    move_core = [
        move(7 + n, eighth(where), eighth(where), partner)
        for n, where in enumerate((t, tminus, tplus, tfar))
    ]
    move_w = [
        move(11, wk_hbm, wkv.at[:, pl.ds(2 * HD, HD)], partner),
        move(12, wv_hbm, wkv.at[:, pl.ds(3 * HD, HD)], partner),
    ]
    move_swap = move(13, swap_out, swap_in, partner)

    @functools.cache
    def gather(r):
        first, second = pl.ds(0, ROWS // 2), pl.ds(ROWS // 2, ROWS // 2)
        plan = (
            (lin.at[r, 0], lin.at[r, 3], zplus),
            (lin.at[r, 0], lin.at[r, 1], zminus),
            (lin.at[r, 3, first], lin.at[r, 2, first], zplus),
            (lin.at[r, 1, second], lin.at[r, 2, second], zminus),
        )
        return [
            remote(src, dst, l_send.at[r, n], l_recv.at[r, n], device)
            for n, (src, dst, device) in enumerate(plan)
        ]

    def gather_relay(r):
        for n in range(2):
            gather(r)[n].wait_recv()
            gather(r)[2 + n].start()

    @functools.cache
    def outer(kind):
        axis, me, _, _ = lines[kind]
        there = 4 * lax.rem(me + 2, 4)
        after = 4 * lax.rem(me + 1, 4)
        before = 4 * lax.rem(me + 3, 4)
        up, down = step(axis, me, 1), step(axis, me, -1)
        plan = (
            (there, up), (there + 2, down), (after + 2, up), (before, down),
            (after, up), (before + 2, down),
        )
        return [
            remote(
                parts.at[kind, pl.ds(start, 2)], near.at[kind, n],
                c_send.at[kind, n], c_recv.at[kind, n], device,
            )
            for n, (start, device) in enumerate(plan)
        ]

    upper, lower = pl.ds(0, TOP), pl.ds(TOP, OWN - TOP)
    stages = (
        ("context", y, mid_half.at[0], far_half.at[0]),
        ("dp", z, mid_half.at[1], far_half.at[1]),
        ("context", y, mid_full.at[0], far_full.at[0]),
        ("context", y, mid_full.at[1], far_full.at[1]),
    )

    @functools.cache
    def inner(s):
        axis, me, mid, far = stages[s]
        there = lax.rem(me + 2, 4)
        after = lax.rem(me + 1, 4)
        before = lax.rem(me + 3, 4)
        up, down = step(axis, me, 1), step(axis, me, -1)
        plan = (
            (there, upper, up), (there, lower, down), (after, lower, up), (before, upper, down),
            (after, upper, up), (before, lower, down),
        )
        return [
            remote(
                mid.at[block, rows], far.at[n, pl.ds(0, rows.size)],
                e_send.at[s, n], e_recv.at[s, n], device,
            )
            for n, (block, rows, device) in enumerate(plan)
        ]

    def stacked(ref, rows):
        return jnp.concatenate([ref[rows, :HD], ref[rows, HD:]], axis=0)

    def forward(i, carry):
        base = pl.multiple_of(i * TILE, TILE)
        rows = pl.ds(base, TILE)
        wide = pl.ds(base, WINDOW)
        low = low_ref[rows, :1] - base
        low = jnp.concatenate([low, low], axis=0)
        row = lax.broadcasted_iota(jnp.int32, (2 * TILE, 1), 0) % TILE
        col = lax.broadcasted_iota(jnp.int32, (2 * TILE, WINDOW), 1)
        scores = nt(stacked(q_ref, rows), keys[wide, :])
        before = jnp.where(col[:, :W] >= low, scores[:, :W], -1e30)
        edge = (col[:, W:] >= low) & (col[:, W:] <= row + W)
        scores = jnp.concatenate([before, jnp.where(edge, scores[:, W:], -1e30)], axis=1)
        top = jnp.max(scores, axis=-1, keepdims=True)
        raised = jnp.exp2((scores - top) * (scale * LOG2E))
        prob = raised * (1.0 / jnp.sum(raised, axis=-1, keepdims=True))
        probs[i] = prob
        half = prob.astype(BF16)
        result = nn(half, values[wide, :]).astype(BF16)
        dvt[:, wide] += nn(stacked(dattn, rows).T, half)
        attn[rows, :HD] = result[:TILE]
        attn[rows, HD:] = result[TILE:]
        return carry

    def backward(i, carry):
        base = pl.multiple_of(i * TILE, TILE)
        rows = pl.ds(base, TILE)
        wide = pl.ds(base, WINDOW)
        grad = stacked(dattn, rows)
        prob = probs[i]
        dprobs = nt(grad, values[wide, :])
        delta = jnp.sum(
            grad.astype(F32) * stacked(attn, rows).astype(F32), axis=-1, keepdims=True
        )
        dscores = (prob * (dprobs - delta) * scale).astype(BF16)
        dq = nn(dscores, keys[wide, :])
        lin[0, 0, rows, :HD] = rotate(dq[:TILE], cos_ref[rows, :], sin_ref[rows, :]).astype(BF16)
        lin[0, 0, rows, HD:] = rotate(
            dq[TILE:], cos_ref[rows, :], sin_ref[rows, :]
        ).astype(BF16)
        dkt[:, wide] += nn(stacked(q_ref, rows).T, dscores)
        return carry

    def outer_multiply():
        right = attn[...]

        def body(i, carry):
            lanes = pl.ds(pl.multiple_of(i * HALF, 128), HALF)
            result = lax.dot_general(
                og[:, lanes], right, (((0,), (0,)), ((), ())), preferred_element_type=F32
            ).astype(BF16)
            for j in range(8):
                rows = slice(OWN * j, OWN * j + OWN)
                parts[0, 8 * i + j] = result[rows, :HD]
                parts[1, 4 * (j % 4) + 2 * i + j // 4] = result[rows, HD:]
            return carry

        lax.fori_loop(0, 2, body, 0)

    def outer_first(kinds, order):
        for n in order:
            for kind in kinds:
                outer(kind)[n].start()

    def outer_second(kind):
        me = lines[kind][1]
        after = 4 * lax.rem(me + 1, 4)
        before = 4 * lax.rem(me + 3, 4)
        for n, start in ((0, after), (1, before + 2)):
            outer(kind)[n].wait_recv()
            where = pl.ds(start, 2)
            parts[kind, where] = (
                parts[kind, where].astype(F32) + near[kind, n].astype(F32)
            ).astype(BF16)
            outer(kind)[4 + n].start()

    def inner_start(s):
        for n in range(4):
            inner(s)[n].start()

    def outer_last(kind):
        me = lines[kind][1]
        for n in (2, 3, 4, 5):
            outer(kind)[n].wait_recv()
        for block in range(4):
            first, second = (4, 3) if block < 2 else (2, 5)
            mid_half[kind, block] = (
                parts[kind, 4 * me + block].astype(F32)
                + near[kind, first, block % 2].astype(F32)
                + near[kind, second, block % 2].astype(F32)
            ).astype(BF16)
        inner_start(kind)

    def inner_multiply(r, *blocks):
        for j in blocks:
            term = lax.dot_general(
                wide_x[j], lin[r, j], (((0,), (0,)), ((), ())), preferred_element_type=F32
            )
            product[...] = term if j == 0 else product[...] + term

    def inner_round(r):
        for block in range(4):
            start = pl.multiple_of(64 * lax.rem(z, 2) + OWN * block, 16)
            mid_full[r, block] = product[pl.ds(start, OWN), :].astype(BF16)
        inner_start(2 + r)

    def inner_second(s):
        _, me, mid, far = stages[s]
        after = lax.rem(me + 1, 4)
        before = lax.rem(me + 3, 4)
        for n, block, rows in ((0, after, upper), (1, before, lower)):
            inner(s)[n].wait_recv()
            mid[block, rows] = (
                mid[block, rows].astype(F32) + far[n, pl.ds(0, rows.size)].astype(F32)
            ).astype(BF16)
            inner(s)[4 + n].start()

    def inner_last(s, outs):
        _, me, mid, far = stages[s]
        for n in (2, 3, 4, 5):
            inner(s)[n].wait_recv()
        for rows, first, second in ((upper, 4, 3), (lower, 2, 5)):
            size = pl.ds(0, rows.size)
            total = (
                mid[me, rows].astype(F32) + far[first, size].astype(F32)
                + far[second, size].astype(F32)
            )
            for out, source, lanes in outs:
                out[rows, lanes] = total[:, source]

    there, after, before = lax.rem(chip + 2, 4), lax.rem(chip + 1, 4), lax.rem(chip + 3, 4)
    pair_copies = [
        remote(ig.at[1 - core, block], pair.at[block], f_send.at[n], f_recv.at[n], partner)
        for n, block in enumerate((there, after, before, chip))
    ]
    ring_x = [
        remote(ig.at[core, block, h], xring.at[n], g_send.at[n], g_recv.at[n], device)
        for n, (block, h, device) in enumerate((
            (there, 0, xplus), (there, 1, xminus), (after, 1, xplus), (before, 0, xminus),
            (after, 0, xplus), (before, 1, xminus),
        ))
    ]

    def query_multiply():
        for h in range(2):
            total = nt(lin[0, 0], wq[pl.ds(h * HALF, HALF), :]).astype(BF16)
            for o in range(8):
                ig[o % 2, o // 2, h] = total[64 * o : 64 * o + 64]

    def core_rows(which):
        return [
            lin[1, 0, pl.ds(pl.multiple_of(64 * (2 * n + which), 64), 64), :] for n in range(4)
        ]

    def key_multiply():
        left = jnp.concatenate(core_rows(core), axis=0)
        left = jnp.concatenate([left, swap_in[...]], axis=1)
        for n in range(4):
            pair_copies[n].wait_recv()
        for h in range(2):
            total = nt(left, wkv[pl.ds(h * HALF, HALF), :])
            for n in range(4):
                ig[core, n, h] = (
                    total[64 * n : 64 * n + 64] + ig[core, n, h].astype(F32)
                    + pair[n, h].astype(F32)
                ).astype(BF16)
            ring_x[h].start()

    def ring_second():
        for n, block in ((0, after), (1, before)):
            ring_x[n].wait_recv()
            ig[core, block, n] = (
                ig[core, block, n].astype(F32) + xring[n].astype(F32)
            ).astype(BF16)
            ring_x[4 + n].start()

    def ring_last():
        for n in (2, 3, 4, 5):
            ring_x[n].wait_recv()
        for h, first, second in ((0, 4, 3), (1, 2, 5)):
            ig_out[:, pl.ds(h * HALF, HALF)] = (
                ig[core, chip, h].astype(F32) + xring[first].astype(F32)
                + xring[second].astype(F32)
            ).astype(BF16)

    for copy in ring_kv[:2] + (load_og, load_wo) + tuple(move_z):
        copy.start()
    for copy in (load_x, load_wk, load_wv) + tuple(move_w):
        copy.start()
    for copy in small[:2]:
        copy.wait()
    lane = lax.broadcasted_iota(jnp.int32, (TILE, HD), 1)
    for n in range(ROWS // TILE):
        rows = slice(TILE * n, TILE * n + TILE)
        place = jnp.broadcast_to(place_ref[n : n + 1, :].astype(F32), (TILE, HD)).T
        angle = place * freq_ref[...]
        cos_ref[rows, :] = jnp.cos(angle)
        sine = jnp.sin(angle)
        sin_ref[rows, :] = jnp.where(lane < HD // 2, sine, -sine)
        row = lax.broadcasted_iota(jnp.int32, (TILE, HD), 0) + TILE * n
        reach = jnp.minimum(place.astype(jnp.int32), W - 1)
        low_ref[rows, :] = jnp.maximum(row - reach + 2 * ROWS, (2 - y) * ROWS)
    dkt[...] = jnp.zeros_like(dkt)
    dvt[...] = jnp.zeros_like(dvt)
    ring_kv[0].wait_send()
    ring_kv[2].start()
    for n in range(2):
        ring_kv[n].wait_recv()
        ring_kv[3 + n].start()
    load_og.wait()
    load_wo.wait()
    dattn[...] = nn(og[...], wq[...]).astype(BF16)
    load_wq.start()
    for copy in small[2:]:
        copy.wait()
    for copy in ring_kv[2:]:
        copy.wait_recv()
    lax.fori_loop(0, 2, forward, 0, unroll=True)
    for copy in move_z:
        copy.wait_recv()
    for copy in move_x[:2] + move_core[:1]:
        copy.start()
    lax.fori_loop(2, ROWS // TILE, forward, 0, unroll=True)
    gout[1] = dvt[:, oldest].astype(BF16)
    gout[2] = dvt[:, middle].astype(BF16)
    for copy in ring_back[1:3]:
        copy.start()
    lax.fori_loop(0, ROWS // TILE, backward, 0, unroll=True)
    gout[0] = dkt[:, oldest].astype(BF16)
    for copy in ring_back[:1] + tuple(gather(0)[:2]):
        copy.start()
    outer_multiply()
    ring_back[1].wait_recv()
    ring_back[4].start()
    load_wq.wait()
    query_multiply()
    for copy in pair_copies:
        copy.start()
    outer_first((0,), (0, 1))
    ring_back[0].wait_recv()
    gin[0] = (gin[0].astype(F32) + dkt[:, middle]).astype(BF16)
    ring_back[3].start()
    load_x.wait()
    inner_multiply(0, 0)
    for n in range(2):
        move_x[n].wait_recv()
        move_x[2 + n].start()
    outer_first((1,), (0,))
    gather_relay(0)
    for copy in ring_back[2:]:
        copy.wait_recv()
    key_grad = (dkt[:, latest] + gin[3].astype(F32)).T
    value_grad = (dvt[:, latest] + gin[2].astype(F32) + gin[4].astype(F32)).T
    lin[1, 0, :, :HD] = rotate(key_grad, cos_ref[...], sin_ref[...]).astype(BF16)
    lin[1, 0, :, HD:] = value_grad.astype(BF16)
    swap_out[...] = jnp.concatenate(core_rows(1 - core), axis=0)
    move_swap.start()
    for copy in move_core[1:3]:
        copy.start()
    for copy in gather(1)[:2]:
        copy.start()
    load_wk.wait()
    load_wv.wait()
    for copy in move_w:
        copy.wait_recv()
    move_swap.wait_recv()
    outer_first((1,), (1, 2, 3))
    key_multiply()
    for copy in move_x[2:]:
        copy.wait_recv()
    move_core[3].start()
    outer_first((0,), (2, 3))
    for copy in move_core + gather(0)[2:]:
        copy.wait_recv()
    inner_multiply(0, 3, 1, 2)
    inner_round(0)
    for n in range(2):
        ring_x[n].wait_send()
        ring_x[2 + n].start()
    gather_relay(1)
    ring_second()
    outer_second(1)
    inner_multiply(1, 0, 3, 1)
    outer_second(0)
    inner_second(2)
    for copy in gather(1)[2:]:
        copy.wait_recv()
    inner_multiply(1, 2)
    inner_round(1)
    outer_last(1)
    outer_last(0)
    inner_second(3)
    inner_second(1)
    inner_second(0)
    every = slice(0, 2 * HD)
    left, right = slice(0, HD), slice(HD, 2 * HD)
    inner_last(2, ((gq_out, every, every),))
    inner_last(3, ((gk_out, left, left), (gv_out, right, left)))
    inner_last(1, ((go_out, left, right),))
    inner_last(0, ((go_out, left, left),))
    ring_last()
    sent = list(ring_kv[1:] + ring_back) + move_z + move_x + move_core + move_w + [move_swap]
    sent += pair_copies + ring_x[2:]
    for s in range(4):
        sent += inner(s)
    for n in range(2):
        sent += gather(n) + outer(n)
    for copy in sent:
        copy.wait_send()


OUTS = (
    jax.ShapeDtypeStruct((64, D), BF16),
    jax.ShapeDtypeStruct((OWN, 2 * HD), F32),
    jax.ShapeDtypeStruct((OWN, HD), F32),
    jax.ShapeDtypeStruct((OWN, HD), F32),
    jax.ShapeDtypeStruct((OWN, 2 * HD), F32),
)


def fused(*operands):
    anywhere = pl.BlockSpec(memory_space=pl.ANY)
    dma = pltpu.SemaphoreType.DMA
    buffers = (
        ((ROWS, HD), jnp.int32),
        ((ROWS, HD), F32),
        ((ROWS, HD), F32),
        ((ROWS, 2 * HD), BF16),
        ((ROWS // TILE, TILE), jnp.int32),
        ((1, HD), F32),
        ((BAND, HD), BF16),
        ((BAND, HD), BF16),
        ((ROWS, HD), BF16),
        ((ROWS, D), BF16),
        ((4, ROWS, SPAN), BF16),
        ((D, 2 * HD), BF16),
        ((D, 4 * HD), BF16),
        ((ROWS, 2 * HD), BF16),
        ((ROWS, 2 * HD), BF16),
        ((2, 4, ROWS, 2 * HD), BF16),
        ((ROWS // 2, 2 * HD), BF16),
        ((ROWS // 2, 2 * HD), BF16),
        ((ROWS // TILE, 2 * TILE, WINDOW), F32),
        ((HD, BAND), F32),
        ((HD, BAND), F32),
        ((3, HD, ROWS), BF16),
        ((5, HD, ROWS), BF16),
        ((SPAN, 2 * HD), F32),
        ((2, 16, OWN, HD), BF16),
        ((2, 6, 2, OWN, HD), BF16),
        ((2, 4, OWN, HD), BF16),
        ((2, 4, OWN, 2 * HD), BF16),
        ((2, 6, TOP, HD), BF16),
        ((2, 6, TOP, 2 * HD), BF16),
        ((2, 4, 2, 64, HALF), BF16),
        ((4, 2, 64, HALF), BF16),
        ((6, 64, HALF), BF16),
    )
    counts = ((5,), (5,), (2, 6), (4, 6), (4,), (6,), (14,), (2, 4))
    return pl.pallas_call(
        fused_kernel,
        out_shape=tuple(pltpu.VMEM(out.shape, out.dtype) for out in OUTS),
        in_specs=[anywhere] * 11,
        out_specs=(pl.BlockSpec(memory_space=pltpu.VMEM),) * 5,
        scratch_shapes=[pltpu.VMEM(*buffer) for buffer in buffers]
        + [dma((13,))]
        + [dma(count) for count in counts for _ in range(2)],
        compiler_params=pltpu.CompilerParams(
            collective_id=0, has_side_effects=True, vmem_limit_bytes=61_000_000
        ),
        name="fused",
    )(*operands)


def finish_kernel(*refs):
    sources, targets, sems = refs[:5], refs[5:10], refs[10]
    stores = [pltpu.make_async_copy(sources[n], targets[n], sems.at[n]) for n in range(5)]
    for store in stores:
        store.start()
    for store in stores:
        store.wait()


def finish(*results):
    anywhere = pl.BlockSpec(memory_space=pl.ANY)
    return pl.pallas_call(
        finish_kernel, out_shape=OUTS,
        in_specs=[pl.BlockSpec(memory_space=pltpu.VMEM)] * 5, out_specs=(anywhere,) * 5,
        scratch_shapes=[pltpu.SemaphoreType.DMA((5,))],
        compiler_params=pltpu.CompilerParams(vmem_limit_bytes=8 << 20),
        name="finish",
    )(*(pltpu.with_memory_space_constraint(result, pltpu.VMEM) for result in results))


def on_device(
    inputs, queries, key_states, value_states, out_grad, positions,
    w_query, w_key, w_value, w_output,
):
    index = np.arange(HD) % (HD // 2)
    freq = jnp.asarray((10000.0 ** (index * (-2.0 / HD))).astype(np.float32)[None, :])
    return finish(
        *fused(
            queries, key_states, value_states, positions.reshape(ROWS // TILE, TILE), freq,
            inputs, out_grad, w_query, w_key, w_value, w_output,
        )
    )


def solution(mesh):
    rows = ("dp", "context")
    return jax.shard_map(
        on_device,
        mesh=mesh,
        in_specs=(
            P(rows, None), P(rows, "tensor"), P(rows, "tensor"), P(rows, "tensor"),
            P(rows, None), P(rows), P(None, "tensor"), P(None, "tensor"),
            P(None, "tensor"), P(None, "tensor"),
        ),
        out_specs=(
            P(("dp", "context", "tensor"), None), P(rows, "tensor"), P(rows, "tensor"),
            P(rows, "tensor"), P(rows, "tensor"),
        ),
        check_vma=False,
    )
```
